256 devices in a mesh: dp: 16 (over z, y_hi), blk: 16 (over y_lo, x, core).
Axes of the slice: x: 4, y: 4 (y_hi: 2, y_lo: 2; y = y_hi * 2 + y_lo), z: 8, core: 2. Of those that a mesh axis runs over, the one named last changes fastest.
Arguments:
- q_raw: bfloat16 [16, 2048, 1536], P('dp', 'blk'), may hold values from -120 to 120
- q_tan: bfloat16 [16, 2048, 1536], P('dp', 'blk'), may hold values from -6 to 6
- k_raw: bfloat16 [16, 2048, 1536], P('dp', 'blk'), may hold values from -120 to 120
- k_tan: bfloat16 [16, 2048, 1536], P('dp', 'blk'), may hold values from -6 to 6
- values: bfloat16 [16, 2048, 1536], P('dp', 'blk'), may hold values from -6 to 6
- values_tan: bfloat16 [16, 2048, 1536], P('dp', 'blk'), may hold values from -6 to 6
- head_scale: float32 [12], replicated, may hold values from 1 to 3
- w_out: bfloat16 [1536, 1536], P('dp'), may hold values from -0.15625 to 0.15625
- gate: float32 [16, 1536], P('dp'), may hold values from 0.5 to 1.5
- gate_tan: float32 [16, 1536], P('dp'), may hold values from -4 to 4
Outputs:
- layer_out: bfloat16 [16, 2048, 1536], P('dp', 'blk')
- layer_tan: bfloat16 [16, 2048, 1536], P('dp', 'blk')
The draws below stay inside these ranges and needn't reach their ends.
All inputs are finite; a program needn't handle non-finite values.
Results may differ from the reference program's by a relative error of at most 0.012.
Values may be sent and summed in bfloat16 or wider, within the bound.
A program may use at most 128 MiB of HBM per device.

```python
import math
import jax
import jax.numpy as jnp
from jax import lax

HEADS = 12
HEAD = 128
DO = 1536
HD = 1536
SEQ = 2048
CLIPS = 16


def scaled_rows(key):
    key_base, key_rows, key_cols = jax.random.split(key, 3)
    base = jax.random.truncated_normal(key_base, -4.0, 4.0, (CLIPS, SEQ, HEADS, HEAD), jnp.float32)
    row_scale = jnp.exp(jax.random.uniform(key_rows, (CLIPS, SEQ, HEADS, 1), jnp.float32, 0.0, math.log(10.0)))
    col_scale = jnp.exp(jax.random.uniform(key_cols, (1, 1, HEADS, HEAD), jnp.float32, math.log(0.3), math.log(3.0)))
    return (base * row_scale * col_scale).reshape(CLIPS, SEQ, HEADS * HEAD)


def draw_q_raw(key, part):
    return scaled_rows(jax.random.fold_in(key, 11)).astype(jnp.bfloat16)


def draw_k_raw(key, part):
    return scaled_rows(jax.random.fold_in(key, 23)).astype(jnp.bfloat16)


def block_levels(rng, dims, pieces, least, top_value):
    gain, own = 1.0, jax.random.fold_in(rng, 6)
    for axis_at, shards_of in pieces:
        draws = jnp.exp(jax.random.uniform(jax.random.fold_in(own, axis_at), (shards_of,), jnp.float32, least / len(pieces), top_value / len(pieces)))
        gain = gain * jnp.repeat(draws, dims[axis_at] // shards_of).reshape([-1 if axis == axis_at else 1 for axis in range(len(dims))])
    return gain


def normal_values(rng, shape, scale, reach, shards=(), held_as=jnp.bfloat16):
    result = scale * jax.random.normal(rng, shape, jnp.float32)
    if shards:
        result = result * block_levels(rng, shape, shards, -0.22, 0.18)
    return jnp.clip(result, -reach, reach).astype(held_as)


def setup_inputs(seed: int = 0) -> dict:
    seeds = jax.random.split(jax.random.key(seed), 11)
    return {
        "q_raw": draw_q_raw(jax.random.fold_in(seeds[10], 71), 0),
        "q_tan": normal_values(seeds[1], (CLIPS, SEQ, HD), 1.0, 6.0, ((0, 16), (1, 16))),
        "k_raw": draw_k_raw(jax.random.fold_in(seeds[10], 71), 0),
        "k_tan": normal_values(seeds[3], (CLIPS, SEQ, HD), 1.0, 6.0, ((0, 16), (1, 16))),
        "values": normal_values(seeds[4], (CLIPS, SEQ, HD), 1.0, 6.0, ((0, 16), (1, 16))),
        "values_tan": normal_values(seeds[5], (CLIPS, SEQ, HD), 1.0, 6.0, ((0, 16), (1, 16))),
        "head_scale": jnp.clip(jnp.exp(jax.random.uniform(seeds[6], (HEADS,), jnp.float32, math.log(1.0), math.log(3.0))), 1.0, 3.0),
        "w_out": normal_values(seeds[7], (HD, DO), HD ** -0.5, 0.15625, ((0, 16),)),
        "gate": jnp.clip(0.5 + 1.0 * jax.random.uniform(seeds[8], (CLIPS, DO), jnp.float32) ** block_levels(seeds[8], (CLIPS, DO), ((0, 16),), -0.2, 0.2), 0.5, 1.5),
        "gate_tan": normal_values(seeds[9], (CLIPS, DO), 1.0, 4.0, ((0, 16),), jnp.float32),
    }


epsilon = 1e-06

def normalize(raw_rows, tan_rows):
    shape = raw_rows.shape[:-1] + (HEADS, HEAD)
    direct = raw_rows.astype(jnp.float32).reshape(shape)
    moving = tan_rows.astype(jnp.float32).reshape(shape)
    recip = lax.rsqrt(lax.optimization_barrier(jnp.mean(direct * direct, -1, keepdims=True)) + epsilon)
    normed = direct * recip
    normed_tan = recip * (moving - normed * lax.optimization_barrier(jnp.mean(normed * moving, -1, keepdims=True)))
    return (normed.astype(jnp.bfloat16), normed_tan.astype(jnp.bfloat16))

def one_clip(q_raw, q_tan, k_raw, k_tan, values, values_tan, head_scale, w_out, gate, gate_tan):
    q_norm, q_dir = normalize(q_raw, q_tan)
    k_norm, k_dir = normalize(k_raw, k_tan)
    val_rows = values.astype(jnp.float32).reshape(SEQ, HEADS, HEAD)
    val_tan = values_tan.astype(jnp.float32).reshape(SEQ, HEADS, HEAD)
    score_scale = (head_scale / math.sqrt(HEAD))[None, :, None]
    q_pair = jnp.concatenate([q_dir, q_norm], -1).astype(jnp.float32)
    k_pair = jnp.concatenate([k_norm, k_dir], -1).astype(jnp.float32)
    scores = jnp.einsum('qhe,khe->qhk', q_norm.astype(jnp.float32), k_norm.astype(jnp.float32)) * score_scale
    slopes = jnp.einsum('qhe,khe->qhk', q_pair, k_pair) * score_scale
    probs = jnp.exp(scores)
    totals = lax.optimization_barrier(jnp.sum(probs, -1))
    moments = lax.optimization_barrier(jnp.sum(probs * slopes, -1))
    prob_half = probs.astype(jnp.bfloat16).astype(jnp.float32)
    slope_half = (probs * slopes).astype(jnp.bfloat16).astype(jnp.float32)
    mixed = jnp.einsum('qhk,khe->qhe', prob_half, val_rows)
    mixed_tan = jnp.einsum('qhk,khe->qhe', slope_half, val_rows) + jnp.einsum('qhk,khe->qhe', prob_half, val_tan)
    attended = (mixed / totals[..., None]).astype(jnp.bfloat16).reshape(SEQ, HD)
    attended_tan = mixed_tan / totals[..., None] - mixed * moments[..., None] / (totals * totals)[..., None]
    attended_tan = attended_tan.astype(jnp.bfloat16).reshape(SEQ, HD)
    stacked = jnp.concatenate([attended, attended_tan], 0)
    projected = jnp.dot(stacked, w_out, preferred_element_type=jnp.float32)
    layer_out = (gate[None, :] * projected[:SEQ]).astype(jnp.bfloat16)
    layer_tan = (gate_tan[None, :] * projected[:SEQ] + gate[None, :] * projected[SEQ:]).astype(jnp.bfloat16)
    return (layer_out, layer_tan)

def reference(q_raw, q_tan, k_raw, k_tan, values, values_tan, head_scale, w_out, gate, gate_tan):

    def step(items):
        return one_clip(items[0], items[1], items[2], items[3], items[4], items[5], head_scale, w_out, items[6], items[7])
    layer_out, layer_tan = lax.map(step, (q_raw, q_tan, k_raw, k_tan, values, values_tan, gate, gate_tan))
    return (layer_out, layer_tan)
```

```python
import math

import jax
import jax.numpy as jnp
from jax import lax
from jax.experimental import pallas as pl
from jax.experimental.pallas import tpu as pltpu
from jax.sharding import PartitionSpec as P

HEADS = 12
HEAD = 128
HD = 1536
ROWS = 128
NX = 4
PER = 3
KEYS = 512
CHUNK = 256
DP_ROWS = 96
HALF = 768
MESH = pl.DeviceIdType.MESH
NT = (((1,), (1,)), ((), ()))
ORDER = (0, 1, 3, 2)
AHEAD = 3

epsilon = 1e-06


def unit_rows(x, dx):
    recip = lax.rsqrt(jnp.mean(x * x, -1, keepdims=True) + epsilon)
    normed = x * recip
    moved = recip * (dx - normed * jnp.mean(normed * dx, -1, keepdims=True))
    return normed.astype(jnp.bfloat16), moved.astype(jnp.bfloat16)


def body(
    q_hbm, qt_hbm, k_hbm, kt_hbm, v_hbm, vt_hbm, scale_ref, w_hbm, out_ref,
    raw, kv, kv_send, qb, q_send, pv, uv, tot, mom, ret, att, w_mine, w_other,
    load_sem, xs, xr, qs, qr, ys, yr, cs, cr, ds, dr, rs, rr,
    w_load, os, orr, ps, pr, ms, mr, ws, wr,
):
    blk, dp = lax.axis_index("blk"), lax.axis_index("dp")
    y, x, c = blk // 8, (blk // 2) % NX, blk % 2
    z, yh = dp // 2, dp % 2

    def at_x(j):
        return {"dp": dp, "blk": y * 8 + ((x + j) % NX) * 2 + c}

    y_peer = {"dp": dp, "blk": (1 - y) * 8 + x * 2 + c}
    c_peer = {"dp": dp, "blk": y * 8 + x * 2 + (1 - c)}
    outer = {"dp": z * 2 + (1 - yh), "blk": (1 - y) * 8 + x * 2 + c}
    z_up = {"dp": ((z + 1) % 8) * 2 + yh, "blk": blk}
    z_down = {"dp": ((z + 7) % 8) * 2 + yh, "blk": blk}

    barrier = pltpu.get_barrier_semaphore()
    peers = [at_x(1), at_x(2), at_x(3), y_peer, c_peer, outer, z_up, z_down]
    for peer in peers:
        pl.semaphore_signal(barrier, inc=1, device_id=peer, device_id_type=MESH)
    loads = []
    for n, src in enumerate((k_hbm, kt_hbm, v_hbm, vt_hbm, q_hbm, qt_hbm)):
        copy = pltpu.make_async_copy(src.at[0], raw.at[n], load_sem.at[n])
        copy.start()
        loads.append(copy)
    my_rows = pl.ds(pl.multiple_of(dp * DP_ROWS, DP_ROWS), DP_ROWS)
    my_cols = pl.ds(pl.multiple_of(c * HALF, HALF), HALF)
    w_copy = pltpu.make_async_copy(w_hbm.at[:, my_cols], w_mine.at[my_rows], w_load)
    w_copy.start()
    pl.semaphore_wait(barrier, len(peers))

    sent = []

    def remote(src, dst, send_sem, recv_sem, peer):
        copy = pltpu.make_async_remote_copy(
            src_ref=src, dst_ref=dst, send_sem=send_sem, recv_sem=recv_sem,
            device_id=peer, device_id_type=MESH,
        )
        copy.start()
        sent.append(copy)
        return copy

    x_in, q_in, y_in, c_in, d_in, r_in = {}, {}, {}, {}, {}, {}

    def forward(i, j):
        own = kv.at[i, j, pl.ds(0, ROWS)]
        y_in[i, j] = remote(own, kv.at[i, j, pl.ds(ROWS, ROWS)], ys.at[i, j], yr.at[i, j], y_peer)
        c_in[i, j] = remote(own, kv.at[i, j, pl.ds(2 * ROWS, ROWS)], cs.at[i, j], cr.at[i, j], c_peer)

    def relay(i, j):
        y_in[i, j].wait_recv()
        d_in[i, j] = remote(
            kv.at[i, j, pl.ds(ROWS, ROWS)], kv.at[i, j, pl.ds(3 * ROWS, ROWS)],
            ds.at[i, j], dr.at[i, j], c_peer,
        )

    def columns(i, j):
        head = PER * ((x + j) % NX) + i
        return pl.ds(pl.multiple_of(head * HEAD, HEAD), HEAD)

    def send_keys(i, j):
        cols = columns(i, j)
        normed, moved = unit_rows(
            raw[0, :, cols].astype(jnp.float32), raw[1, :, cols].astype(jnp.float32)
        )
        dst = kv.at[i, 0, pl.ds(0, ROWS)] if j == 0 else kv_send.at[i, j - 1]
        dst[:, 0:128] = normed
        dst[:, 128:256] = moved
        dst[:, 256:384] = raw[2, :, cols]
        dst[:, 384:512] = raw[3, :, cols]
        if j == 0:
            forward(i, 0)
        else:
            x_in[i, j] = remote(
                dst, kv.at[i, j, pl.ds(0, ROWS)], xs.at[i, j], xr.at[i, j], at_x(j)
            )

    def send_queries(i, j):
        cols = columns(i, j)
        normed, moved = unit_rows(
            raw[4, :, cols].astype(jnp.float32), raw[5, :, cols].astype(jnp.float32)
        )
        dst = qb.at[i, pl.ds(0, ROWS)] if j == 0 else q_send.at[i, j - 1]
        dst[:, 0:128] = moved
        dst[:, 128:256] = normed
        if j != 0:
            q_in[i, j] = remote(
                dst, qb.at[i, pl.ds(j * ROWS, ROWS)], qs.at[i, j], qr.at[i, j], at_x(j)
            )

    w_copy.wait()
    outer_in = remote(w_mine.at[my_rows], w_mine.at[my_rows], os, orr, outer)

    for n in range(4):
        loads[n].wait()
    for j in ORDER:
        send_keys(0, j)
    loads[4].wait()
    loads[5].wait()
    for j in ORDER:
        send_queries(0, j)

    def w_block(step):
        block = (z + step + 8) % 8
        return pl.ds(pl.multiple_of(block * 192, 192), 192)

    w_in = []
    up_in, down_in = {}, {}

    def w_pass(step):
        if step == 0:
            outer_in.wait_recv()
        else:
            up_in[step].wait_recv()
            if step <= 3:
                down_in[step].wait_recv()
        low = w_block(-step)
        if step < 4:
            up_in[step + 1] = remote(
                w_mine.at[low], w_mine.at[low], ps.at[step], pr.at[step], z_up
            )
        w_in.append(remote(w_mine.at[low], w_other.at[low], ws.at[step], wr.at[step], c_peer))
        if step <= 3:
            high = w_block(step)
            if step < 3:
                down_in[step + 1] = remote(
                    w_mine.at[high], w_mine.at[high], ms.at[step], mr.at[step], z_down
                )
            if step > 0:
                w_in.append(
                    remote(w_mine.at[high], w_other.at[high], ws.at[4 + step], wr.at[4 + step], c_peer)
                )

    w_pass(0)
    for i in range(1, PER):
        for j in ORDER:
            send_keys(i, j)
        for j in ORDER:
            send_queries(i, j)

    steps = [(i, j) for i in range(PER) for j in ORDER]
    passed = 0

    def pass_up_to(n):
        nonlocal passed
        while passed < min(n, len(steps)):
            i, j = steps[passed]
            if j != 0:
                x_in[i, j].wait_recv()
                forward(i, j)
            passed += 1

    def attend(i, j):
        scale = scale_ref[PER * x + i] * (1.0 / math.sqrt(HEAD))
        rate = scale * math.log2(math.e)

        def chunk(n, carry):
            rows = pl.ds(pl.multiple_of(n * CHUNK, CHUNK), CHUNK)
            queries = qb[i, rows, :]
            scores = lax.dot_general(
                queries[:, 128:256], kv[i, j, :, 0:128], NT, preferred_element_type=jnp.float32
            )
            slopes = lax.dot_general(
                queries, kv[i, j, :, 0:256], NT, preferred_element_type=jnp.float32
            )
            probs = jnp.exp2(scores * rate)
            weighted = probs * (slopes * scale)
            p_sum = probs[:, 0:128]
            w_sum = weighted[:, 0:128]
            for part in range(1, KEYS // 128):
                p_sum = p_sum + probs[:, part * 128 : (part + 1) * 128]
                w_sum = w_sum + weighted[:, part * 128 : (part + 1) * 128]
            p_mix = jnp.dot(
                probs.astype(jnp.bfloat16), kv[i, j, :, 256:512], preferred_element_type=jnp.float32
            )
            w_mix = jnp.dot(
                weighted.astype(jnp.bfloat16), kv[i, j, :, 256:384], preferred_element_type=jnp.float32
            )
            if j == 0:
                tot[rows, :] = p_sum
                mom[rows, :] = w_sum
                pv[rows, :] = p_mix
                uv[rows, :] = w_mix
            else:
                tot[rows, :] += p_sum
                mom[rows, :] += w_sum
                pv[rows, :] += p_mix
                uv[rows, :] += w_mix
            return carry

        lax.fori_loop(0, KEYS // CHUNK, chunk, 0)

    def finish(i):
        head = PER * x + i
        cols = pl.ds(pl.multiple_of(head * HEAD, HEAD), HEAD)
        for j in (2, 1, 3, 0):
            rows = pl.ds(j * ROWS, ROWS)
            inv = 1.0 / jnp.sum(tot[rows, :], -1, keepdims=True)
            moment = jnp.sum(mom[rows, :], -1, keepdims=True) * inv
            mixed = pv[rows, 0:128]
            main = (mixed * inv).astype(jnp.bfloat16)
            tangent = ((uv[rows, :] + pv[rows, 128:256] - mixed * moment) * inv).astype(jnp.bfloat16)
            if j == 0:
                att[0:ROWS, cols] = main
                att[ROWS : 2 * ROWS, cols] = tangent
            else:
                ret[i, j - 1, 0:ROWS, :] = main
                ret[i, j - 1, ROWS : 2 * ROWS, :] = tangent
                r_in[i, j] = remote(
                    ret.at[i, j - 1], att.at[:, cols], rs.at[i, j], rr.at[i, j], at_x(NX - j)
                )

    w_steps = {3: 1, 5: 2, 8: 3, 10: 4}
    pass_up_to(AHEAD)
    relay(*steps[0])
    for n, (i, j) in enumerate(steps):
        pass_up_to(n + 1 + AHEAD)
        if n in w_steps:
            w_pass(w_steps[n])
        if n + 1 < len(steps):
            relay(*steps[n + 1])
        if j == 0:
            for other in ORDER[1:]:
                q_in[i, other].wait_recv()
        c_in[i, j].wait_recv()
        d_in[i, j].wait_recv()
        attend(i, j)
        if j == ORDER[-1]:
            finish(i)

    for copy in w_in:
        copy.wait_recv()
    for copy in r_in.values():
        copy.wait_recv()

    def project(n, carry):
        for half, offset in ((w_mine, c), (w_other, 1 - c)):
            cols = pl.ds(pl.multiple_of(offset * HALF + n * 256, 256), 256)
            out_ref[:, cols] = jnp.dot(
                att[...], half[:, pl.ds(pl.multiple_of(n * 256, 256), 256)],
                preferred_element_type=jnp.float32,
            )
        return carry

    lax.fori_loop(0, HALF // 256, project, 0)
    for copy in sent:
        copy.wait_send()


def attention(q_raw, q_tan, k_raw, k_tan, values, values_tan, head_scale, w_out):
    bf16, f32 = jnp.bfloat16, jnp.float32
    dma = pltpu.SemaphoreType.DMA
    any_spec = pl.BlockSpec(memory_space=pl.ANY)
    return pl.pallas_call(
        body,
        out_shape=jax.ShapeDtypeStruct((2 * ROWS, HD), f32),
        in_specs=[any_spec] * 6 + [pl.BlockSpec(memory_space=pltpu.SMEM), any_spec],
        out_specs=pl.BlockSpec(memory_space=pltpu.VMEM),
        scratch_shapes=[
            pltpu.VMEM((6, ROWS, HD), bf16),
            pltpu.VMEM((PER, NX, KEYS, 512), bf16),
            pltpu.VMEM((PER, NX - 1, ROWS, 512), bf16),
            pltpu.VMEM((PER, KEYS, 256), bf16),
            pltpu.VMEM((PER, NX - 1, ROWS, 256), bf16),
            pltpu.VMEM((KEYS, 256), f32),
            pltpu.VMEM((KEYS, 128), f32),
            pltpu.VMEM((KEYS, 128), f32),
            pltpu.VMEM((KEYS, 128), f32),
            pltpu.VMEM((PER, NX - 1, 2 * ROWS, HEAD), bf16),
            pltpu.VMEM((2 * ROWS, HD), bf16),
            pltpu.VMEM((HD, HALF), bf16),
            pltpu.VMEM((HD, HALF), bf16),
            dma((6,)),
        ]
        + [dma((PER, NX))] * 12
        + [dma, dma, dma]
        + [dma((4,)), dma((4,)), dma((3,)), dma((3,)), dma((8,)), dma((8,))],
        compiler_params=pltpu.CompilerParams(
            collective_id=0, has_side_effects=True, vmem_limit_bytes=48 * 1024 * 1024
        ),
        cost_estimate=pl.CostEstimate(
            flops=7_000_000_000, bytes_accessed=10_000_000, transcendentals=3_200_000
        ),
        name="attention",
    )(q_raw, q_tan, k_raw, k_tan, values, values_tan, head_scale, w_out)


def shards(q_raw, q_tan, k_raw, k_tan, values, values_tan, head_scale, w_out, gate, gate_tan):
    projected = attention(q_raw, q_tan, k_raw, k_tan, values, values_tan, head_scale, w_out)
    layer_out = (gate * projected[:ROWS]).astype(jnp.bfloat16)
    layer_tan = (gate_tan * projected[:ROWS] + gate * projected[ROWS:]).astype(jnp.bfloat16)
    return (layer_out[None], layer_tan[None])


def solution(mesh):
    rows = P("dp", "blk", None)
    return jax.shard_map(
        shards,
        mesh=mesh,
        in_specs=(rows,) * 6 + (P(), P("dp", None), P("dp", None), P("dp", None)),
        out_specs=(rows, rows),
        check_vma=False,
    )
```

```python
import math

import jax
import jax.numpy as jnp
from jax import lax
from jax.experimental import pallas as pl
from jax.experimental.pallas import tpu as pltpu
from jax.sharding import PartitionSpec as P

HEADS = 12
HEAD = 128
HD = 1536
ROWS = 128
NX = 4
PER = 3
KEYS = 512
DP_ROWS = 96
HALF = 768
MESH = pl.DeviceIdType.MESH
NT = (((1,), (1,)), ((), ()))
ORDER = (0, 1, 3, 2)
AHEAD = 3
W_LAG = 2

epsilon = 1e-06


def unit_rows(x, dx):
    recip = lax.rsqrt(jnp.mean(x * x, -1, keepdims=True) + epsilon)
    normed = x * recip
    moved = recip * (dx - normed * jnp.mean(normed * dx, -1, keepdims=True))
    return normed.astype(jnp.bfloat16), moved.astype(jnp.bfloat16)


def body(
    q_hbm, qt_hbm, k_hbm, kt_hbm, v_hbm, vt_hbm, w_hbm, gate_hbm, gate_tan_hbm, scale_hbm, out_ref, tan_ref,
    raw, gates, scale_ref, kv, kv_send, qb, q_send, pv, uv, tot, mom, ret, att, w_mine, w_other,
    load_sem, xs, xr, qs, qr, ys, yr, cs, cr, ds, dr, rs, rr,
    g_load, s_load, w_load, os, orr, ps, pr, ms, mr, ws, wr,
):
    blk, dp = lax.axis_index("blk"), lax.axis_index("dp")
    y, x, c = blk // 8, (blk // 2) % NX, blk % 2
    z, yh = dp // 2, dp % 2

    def at_x(j):
        return {"dp": dp, "blk": y * 8 + ((x + j) % NX) * 2 + c}

    y_peer = {"dp": dp, "blk": (1 - y) * 8 + x * 2 + c}
    c_peer = {"dp": dp, "blk": y * 8 + x * 2 + (1 - c)}
    outer = {"dp": z * 2 + (1 - yh), "blk": (1 - y) * 8 + x * 2 + c}
    z_up = {"dp": ((z + 1) % 8) * 2 + yh, "blk": blk}
    z_down = {"dp": ((z + 7) % 8) * 2 + yh, "blk": blk}

    barrier = pltpu.get_barrier_semaphore()
    peers = [at_x(1), at_x(2), at_x(3), y_peer, c_peer, outer, z_up, z_down]
    for peer in peers:
        pl.semaphore_signal(barrier, inc=1, device_id=peer, device_id_type=MESH)
    loads = []
    for n, src in enumerate((k_hbm, kt_hbm, v_hbm, vt_hbm, q_hbm, qt_hbm)):
        copy = pltpu.make_async_copy(src.at[0], raw.at[n], load_sem.at[n])
        copy.start()
        loads.append(copy)
    my_rows = pl.ds(pl.multiple_of(dp * DP_ROWS, DP_ROWS), DP_ROWS)
    my_cols = pl.ds(pl.multiple_of(c * HALF, HALF), HALF)
    w_copy = pltpu.make_async_copy(w_hbm.at[:, my_cols], w_mine.at[my_rows], w_load)
    w_copy.start()
    for n, src in enumerate((gate_hbm, gate_tan_hbm)):
        copy = pltpu.make_async_copy(src, gates.at[pl.ds(n, 1)], g_load.at[n])
        copy.start()
        loads.append(copy)
    s_copy = pltpu.make_async_copy(scale_hbm, scale_ref, s_load)
    s_copy.start()
    pl.semaphore_wait(barrier, len(peers))

    sent = []

    def remote(src, dst, send_sem, recv_sem, peer):
        copy = pltpu.make_async_remote_copy(
            src_ref=src, dst_ref=dst, send_sem=send_sem, recv_sem=recv_sem,
            device_id=peer, device_id_type=MESH,
        )
        copy.start()
        sent.append(copy)
        return copy

    x_in, q_in, y_in, c_in, d_in, r_in = {}, {}, {}, {}, {}, {}

    def forward(i, j):
        own = kv.at[i, j, pl.ds(0, ROWS)]
        y_in[i, j] = remote(own, kv.at[i, j, pl.ds(ROWS, ROWS)], ys.at[i, j], yr.at[i, j], y_peer)
        c_in[i, j] = remote(own, kv.at[i, j, pl.ds(2 * ROWS, ROWS)], cs.at[i, j], cr.at[i, j], c_peer)

    def relay(i, j):
        y_in[i, j].wait_recv()
        d_in[i, j] = remote(
            kv.at[i, j, pl.ds(ROWS, ROWS)], kv.at[i, j, pl.ds(3 * ROWS, ROWS)],
            ds.at[i, j], dr.at[i, j], c_peer,
        )

    def columns(i, j):
        head = PER * ((x + j) % NX) + i
        return pl.ds(pl.multiple_of(head * HEAD, HEAD), HEAD)

    def send_keys(i, j):
        cols = columns(i, j)
        normed, moved = unit_rows(
            raw[0, :, cols].astype(jnp.float32), raw[1, :, cols].astype(jnp.float32)
        )
        dst = kv.at[i, 0, pl.ds(0, ROWS)] if j == 0 else kv_send.at[i, j - 1]
        dst[:, 0:128] = normed
        dst[:, 128:256] = moved
        dst[:, 256:384] = raw[2, :, cols]
        dst[:, 384:512] = raw[3, :, cols]
        if j == 0:
            forward(i, 0)
        else:
            x_in[i, j] = remote(
                dst, kv.at[i, j, pl.ds(0, ROWS)], xs.at[i, j], xr.at[i, j], at_x(j)
            )

    def send_queries(i, j):
        cols = columns(i, j)
        normed, moved = unit_rows(
            raw[4, :, cols].astype(jnp.float32), raw[5, :, cols].astype(jnp.float32)
        )
        dst = qb.at[i, pl.ds(0, ROWS)] if j == 0 else q_send.at[i, j - 1]
        dst[:, 0:128] = moved
        dst[:, 128:256] = normed
        if j != 0:
            q_in[i, j] = remote(
                dst, qb.at[i, pl.ds(j * ROWS, ROWS)], qs.at[i, j], qr.at[i, j], at_x(j)
            )

    def piece(distance, other):
        row = (((z + distance + 8) % 8) * 2 + (1 - yh if other else yh)) * DP_ROWS
        return w_mine.at[pl.ds(pl.multiple_of(row, DP_ROWS), DP_ROWS)], w_other.at[
            pl.ds(pl.multiple_of(row, DP_ROWS), DP_ROWS)
        ]

    up_in, down_in, w_in = {}, {}, []

    def w_send(distance, other, going):
        if going > 0:
            n = 2 * distance + other
            here = piece(-distance, other)[0]
            up_in[n] = remote(here, here, ps.at[n], pr.at[n], z_up)
        else:
            n = 2 * distance + other if distance < 3 else 6
            here = piece(distance, other)[0]
            down_in[n] = remote(here, here, ms.at[n], mr.at[n], z_down)

    def w_share(distance, other, n):
        here, there = piece(distance, other)
        w_in.append(remote(here, there, ws.at[n], wr.at[n], c_peer))

    def w_pass(n):
        up_in[n].wait_recv()
        down_in[n].wait_recv()
        distance, other = n // 2 + 1, n % 2
        if n < 5:
            w_send(distance, other, 1)
        if n < 4:
            w_send(distance, other, -1)
        if n == 5:
            w_send(3, 1, -1)
        w_share(-distance, other, 2 + n)
        w_share(distance, other if n < 6 else 1, 9 + n)

    for n in range(4):
        loads[n].wait()
    for j in ORDER:
        send_keys(0, j)
    w_copy.wait()
    outer_in = remote(w_mine.at[my_rows], w_mine.at[my_rows], os, orr, outer)
    w_send(0, 0, 1)
    w_send(0, 0, -1)
    loads[4].wait()
    loads[5].wait()
    for j in ORDER:
        send_queries(0, j)

    for i in range(1, PER):
        for j in ORDER:
            send_keys(i, j)
        for j in ORDER:
            send_queries(i, j)
    outer_in.wait_recv()
    w_send(0, 1, 1)
    w_send(0, 1, -1)
    w_share(0, 0, 0)
    w_share(0, 1, 1)

    steps = [(i, j) for i in range(PER) for j in ORDER]
    passed = 0

    def pass_up_to(n):
        nonlocal passed
        while passed < min(n, len(steps)):
            i, j = steps[passed]
            if j != 0:
                x_in[i, j].wait_recv()
                forward(i, j)
            passed += 1

    def attend(i, j):
        scale = scale_ref[PER * x + i] * (1.0 / math.sqrt(HEAD))
        rate = scale * math.log2(math.e)

        scores = lax.dot_general(
            qb[i, :, 128:256], kv[i, j, :, 0:128], NT, preferred_element_type=jnp.float32
        )
        slopes = lax.dot_general(
            qb[i], kv[i, j, :, 0:256], NT, preferred_element_type=jnp.float32
        )
        probs = jnp.exp2(scores * rate)
        weighted = probs * (slopes * scale)
        p_sum = probs[:, 0:128]
        w_sum = weighted[:, 0:128]
        for part in range(1, KEYS // 128):
            p_sum = p_sum + probs[:, part * 128 : (part + 1) * 128]
            w_sum = w_sum + weighted[:, part * 128 : (part + 1) * 128]
        p_mix = jnp.dot(
            probs.astype(jnp.bfloat16), kv[i, j, :, 256:512], preferred_element_type=jnp.float32
        )
        w_mix = jnp.dot(
            weighted.astype(jnp.bfloat16), kv[i, j, :, 256:384], preferred_element_type=jnp.float32
        )
        if j == 0:
            tot[...] = p_sum
            mom[...] = w_sum
            pv[...] = p_mix
            uv[...] = w_mix
        else:
            tot[...] += p_sum
            mom[...] += w_sum
            pv[...] += p_mix
            uv[...] += w_mix

    def finish(i):
        head = PER * x + i
        cols = pl.ds(pl.multiple_of(head * HEAD, HEAD), HEAD)
        for j in (2, 1, 3, 0):
            rows = pl.ds(j * ROWS, ROWS)
            inv = 1.0 / jnp.sum(tot[rows, :], -1, keepdims=True)
            moment = jnp.sum(mom[rows, :], -1, keepdims=True) * inv
            mixed = pv[rows, 0:128]
            main = (mixed * inv).astype(jnp.bfloat16)
            tangent = ((uv[rows, :] + pv[rows, 128:256] - mixed * moment) * inv).astype(jnp.bfloat16)
            if j == 0:
                att[0:ROWS, cols] = main
                att[ROWS : 2 * ROWS, cols] = tangent
            else:
                ret[i, j - 1, 0:ROWS, :] = main
                ret[i, j - 1, ROWS : 2 * ROWS, :] = tangent
                r_in[i, j] = remote(
                    ret.at[i, j - 1], att.at[:, cols], rs.at[i, j], rr.at[i, j], at_x(NX - j)
                )

    s_copy.wait()
    pass_up_to(AHEAD)
    relay(*steps[0])
    for n, (i, j) in enumerate(steps):
        pass_up_to(n + 1 + AHEAD)
        if 0 <= n - W_LAG < 7:
            w_pass(n - W_LAG)
        if n + 1 < len(steps):
            relay(*steps[n + 1])
        if j == 0:
            for other in ORDER[1:]:
                q_in[i, other].wait_recv()
        c_in[i, j].wait_recv()
        d_in[i, j].wait_recv()
        attend(i, j)
        if j == ORDER[-1]:
            finish(i)

    loads[6].wait()
    loads[7].wait()
    for copy in w_in:
        copy.wait_recv()
    for copy in r_in.values():
        copy.wait_recv()

    def project(n, carry):
        for half, offset in ((w_mine, c), (w_other, 1 - c)):
            cols = pl.ds(pl.multiple_of(offset * HALF + n * 256, 256), 256)
            projected = jnp.dot(
                att[...], half[:, pl.ds(pl.multiple_of(n * 256, 256), 256)],
                preferred_element_type=jnp.float32,
            )
            gate, gate_tan = gates[0:1, cols], gates[1:2, cols]
            out_ref[:, cols] = gate * projected[0:ROWS]
            tan_ref[:, cols] = gate_tan * projected[0:ROWS] + gate * projected[ROWS:]
        return carry

    lax.fori_loop(0, HALF // 256, project, 0)
    for copy in sent:
        copy.wait_send()


def attention(q_raw, q_tan, k_raw, k_tan, values, values_tan, w_out, gate, gate_tan, head_scale):
    bf16, f32 = jnp.bfloat16, jnp.float32
    dma = pltpu.SemaphoreType.DMA
    any_spec = pl.BlockSpec(memory_space=pl.ANY)
    return pl.pallas_call(
        body,
        out_shape=[jax.ShapeDtypeStruct((ROWS, HD), f32)] * 2,
        in_specs=[any_spec] * 10,
        out_specs=[pl.BlockSpec(memory_space=pltpu.VMEM)] * 2,
        scratch_shapes=[
            pltpu.VMEM((6, ROWS, HD), bf16),
            pltpu.VMEM((2, HD), f32),
            pltpu.SMEM((HEADS,), f32),
            pltpu.VMEM((PER, NX, KEYS, 512), bf16),
            pltpu.VMEM((PER, NX - 1, ROWS, 512), bf16),
            pltpu.VMEM((PER, KEYS, 256), bf16),
            pltpu.VMEM((PER, NX - 1, ROWS, 256), bf16),
            pltpu.VMEM((KEYS, 256), f32),
            pltpu.VMEM((KEYS, 128), f32),
            pltpu.VMEM((KEYS, 128), f32),
            pltpu.VMEM((KEYS, 128), f32),
            pltpu.VMEM((PER, NX - 1, 2 * ROWS, HEAD), bf16),
            pltpu.VMEM((2 * ROWS, HD), bf16),
            pltpu.VMEM((HD, HALF), bf16),
            pltpu.VMEM((HD, HALF), bf16),
            dma((6,)),
        ]
        + [dma((PER, NX))] * 12
        + [dma((2,)), dma, dma, dma, dma]
        + [dma((7,)), dma((7,)), dma((7,)), dma((7,)), dma((16,)), dma((16,))],
        compiler_params=pltpu.CompilerParams(
            collective_id=0, has_side_effects=True, vmem_limit_bytes=48 * 1024 * 1024
        ),
        cost_estimate=pl.CostEstimate(
            flops=7_000_000_000, bytes_accessed=10_000_000, transcendentals=3_200_000
        ),
        name="attention",
    )(q_raw, q_tan, k_raw, k_tan, values, values_tan, w_out, gate, gate_tan, head_scale)


def shards(q_raw, q_tan, k_raw, k_tan, values, values_tan, head_scale, w_out, gate, gate_tan):
    arrays = (q_raw, q_tan, k_raw, k_tan, values, values_tan, w_out, gate, gate_tan, head_scale)
    main, tangent = attention(
        *(pltpu.with_memory_space_constraint(array, pltpu.HBM) for array in arrays)
    )
    return (main.astype(jnp.bfloat16)[None], tangent.astype(jnp.bfloat16)[None])


def solution(mesh):
    rows = P("dp", "blk", None)
    return jax.shard_map(
        shards,
        mesh=mesh,
        in_specs=(rows,) * 6 + (P(), P("dp", None), P("dp", None), P("dp", None)),
        out_specs=(rows, rows),
        check_vma=False,
    )
```

```python
import math

import jax
import jax.numpy as jnp
from jax import lax
from jax.experimental import pallas as pl
from jax.experimental.pallas import tpu as pltpu
from jax.sharding import PartitionSpec as P

HEADS = 12
HEAD = 128
HD = 1536
ROWS = 128
NX = 4
PER = 3
KEYS = 512
DP_ROWS = 96
HALF = 768
MESH = pl.DeviceIdType.MESH
NT = (((1,), (1,)), ((), ()))
ORDER = (0, 1, 3, 2)
AHEAD = 3
W_OTHER = 0
W_PLAN = {1: (0,), 3: (1,), 5: (2,), 6: (3,), 7: (4,), 9: (5,), 10: (6,)}

epsilon = 1e-06


def unit_rows(x, dx):
    recip = lax.rsqrt(jnp.mean(x * x, -1, keepdims=True) + epsilon)
    normed = x * recip
    moved = recip * (dx - normed * jnp.mean(normed * dx, -1, keepdims=True))
    return normed.astype(jnp.bfloat16), moved.astype(jnp.bfloat16)


def body(
    q_hbm, qt_hbm, k_hbm, kt_hbm, v_hbm, vt_hbm, w_hbm, gate_hbm, gate_tan_hbm, scale_hbm, out_ref, tan_ref,
    raw, gates, scale_ref, kv, kv_send, qb, q_send, pv, uv, tot, mom, ret, att, part, w_mine, w_other,
    load_sem, xs, xr, qs, qr, ys, yr, cs, cr, ds, dr, rs, rr,
    go_clip, go_w, g_load, s_load, w_load, os, orr, ps, pr, ms, mr, ws, wr,
):
    blk, dp = lax.axis_index("blk"), lax.axis_index("dp")
    y, x, c = blk // 8, (blk // 2) % NX, blk % 2
    z, yh = dp // 2, dp % 2

    def at_x(j):
        return {"dp": dp, "blk": y * 8 + ((x + j) % NX) * 2 + c}

    y_peer = {"dp": dp, "blk": (1 - y) * 8 + x * 2 + c}
    c_peer = {"dp": dp, "blk": y * 8 + x * 2 + (1 - c)}
    outer = {"dp": z * 2 + (1 - yh), "blk": (1 - y) * 8 + x * 2 + c}
    z_up = {"dp": ((z + 1) % 8) * 2 + yh, "blk": blk}
    z_down = {"dp": ((z + 7) % 8) * 2 + yh, "blk": blk}

    barrier = pltpu.get_barrier_semaphore()

    def greet(peer):
        pl.semaphore_signal(barrier, inc=1, device_id=peer, device_id_type=MESH)

    for j in range(1, NX):
        greet({"dp": dp, "blk": y * 8 + ((x + j) % NX) * 2})
    greet({"dp": dp, "blk": (1 - y) * 8 + x * 2})
    pl.when(c == 1)(lambda: greet({"dp": dp, "blk": y * 8 + x * 2}))
    greet({"dp": z * 2 + (1 - yh), "blk": (1 - y) * 8 + x * 2 + 1})
    greet({"dp": ((z + 1) % 8) * 2 + yh, "blk": y * 8 + x * 2 + 1})
    greet({"dp": ((z + 7) % 8) * 2 + yh, "blk": y * 8 + x * 2 + 1})
    loads = []
    for n, src in enumerate((k_hbm, kt_hbm, v_hbm, vt_hbm, q_hbm, qt_hbm)):
        copy = pltpu.make_async_copy(src.at[0], raw.at[n], load_sem.at[n])
        copy.start()
        loads.append(copy)
    my_rows = pl.ds(pl.multiple_of(dp * DP_ROWS, DP_ROWS), DP_ROWS)
    my_cols = pl.ds(pl.multiple_of(c * HALF, HALF), HALF)
    w_copy = pltpu.make_async_copy(w_hbm.at[:, my_cols], w_mine.at[my_rows], w_load)
    w_copy.start()
    for n, src in enumerate((gate_hbm, gate_tan_hbm)):
        copy = pltpu.make_async_copy(src, gates.at[pl.ds(n, 1)], g_load.at[n])
        copy.start()
        loads.append(copy)
    s_copy = pltpu.make_async_copy(scale_hbm, scale_ref, s_load)
    s_copy.start()

    @pl.when(c == 0)
    def _():
        pl.semaphore_wait(barrier, 9)
        pl.semaphore_signal(go_clip, inc=1, device_id=c_peer, device_id_type=MESH)

    @pl.when(c == 1)
    def _():
        pl.semaphore_wait(go_clip, 1)


    sent = []

    def remote(src, dst, send_sem, recv_sem, peer):
        copy = pltpu.make_async_remote_copy(
            src_ref=src, dst_ref=dst, send_sem=send_sem, recv_sem=recv_sem,
            device_id=peer, device_id_type=MESH,
        )
        copy.start()
        sent.append(copy)
        return copy

    x_in, q_in, y_in, c_in, d_in, r_in = {}, {}, {}, {}, {}, {}

    def forward(i, j):
        own = kv.at[i, j, pl.ds(0, ROWS)]
        y_in[i, j] = remote(own, kv.at[i, j, pl.ds(ROWS, ROWS)], ys.at[i, j], yr.at[i, j], y_peer)
        c_in[i, j] = remote(own, kv.at[i, j, pl.ds(2 * ROWS, ROWS)], cs.at[i, j], cr.at[i, j], c_peer)

    def relay(i, j):
        y_in[i, j].wait_recv()
        d_in[i, j] = remote(
            kv.at[i, j, pl.ds(ROWS, ROWS)], kv.at[i, j, pl.ds(3 * ROWS, ROWS)],
            ds.at[i, j], dr.at[i, j], c_peer,
        )

    def columns(i, j):
        head = PER * ((x + j) % NX) + i
        return pl.ds(pl.multiple_of(head * HEAD, HEAD), HEAD)

    def send_keys(i, j):
        cols = columns(i, j)
        normed, moved = unit_rows(
            raw[0, :, cols].astype(jnp.float32), raw[1, :, cols].astype(jnp.float32)
        )
        dst = kv.at[i, 0, pl.ds(0, ROWS)] if j == 0 else kv_send.at[i, j - 1]
        dst[:, 0:128] = normed
        dst[:, 128:256] = moved
        dst[:, 256:384] = raw[2, :, cols]
        dst[:, 384:512] = raw[3, :, cols]
        if j == 0:
            forward(i, 0)
        else:
            x_in[i, j] = remote(
                dst, kv.at[i, j, pl.ds(0, ROWS)], xs.at[i, j], xr.at[i, j], at_x(j)
            )

    def send_queries(i, j):
        cols = columns(i, j)
        normed, moved = unit_rows(
            raw[4, :, cols].astype(jnp.float32), raw[5, :, cols].astype(jnp.float32)
        )
        dst = qb.at[i, pl.ds(0, ROWS)] if j == 0 else q_send.at[i, j - 1]
        dst[:, 0:128] = moved
        dst[:, 128:256] = normed
        if j != 0:
            q_in[i, j] = remote(
                dst, qb.at[i, pl.ds(j * ROWS, ROWS)], qs.at[i, j], qr.at[i, j], at_x(j)
            )

    def piece(distance, other):
        row = (((z + distance + 8) % 8) * 2 + (1 - yh if other else yh)) * DP_ROWS
        return w_mine.at[pl.ds(pl.multiple_of(row, DP_ROWS), DP_ROWS)], w_other.at[
            pl.ds(pl.multiple_of(row, DP_ROWS), DP_ROWS)
        ]

    up_in, down_in, w_in = {}, {}, []

    def w_send(distance, other, going):
        if going > 0:
            n = 2 * distance + other
            here = piece(-distance, other)[0]
            up_in[n] = remote(here, here, ps.at[n], pr.at[n], z_up)
        else:
            n = 2 * distance + other if distance < 3 else 6
            here = piece(distance, other)[0]
            down_in[n] = remote(here, here, ms.at[n], mr.at[n], z_down)

    def w_share(distance, other, n):
        here, there = piece(distance, other)
        w_in.append(remote(here, there, ws.at[n], wr.at[n], c_peer))

    def w_pass(n):
        up_in[n].wait_recv()
        down_in[n].wait_recv()
        distance, other = n // 2 + 1, n % 2
        if n < 5:
            w_send(distance, other, 1)
        if n < 4:
            w_send(distance, other, -1)
        if n == 5:
            w_send(3, 1, -1)
        w_share(-distance, other, 2 + n)
        w_share(distance, other if n < 6 else 1, 9 + n)

    for n in range(4):
        loads[n].wait()
    for j in ORDER:
        send_keys(0, j)
    loads[4].wait()
    loads[5].wait()
    for j in ORDER:
        send_queries(0, j)

    for i in range(1, PER):
        for j in ORDER:
            send_keys(i, j)
        for j in ORDER:
            send_queries(i, j)
    @pl.when(c == 1)
    def _():
        pl.semaphore_wait(barrier, 6)
        pl.semaphore_signal(go_w, inc=1, device_id=c_peer, device_id_type=MESH)

    @pl.when(c == 0)
    def _():
        pl.semaphore_wait(go_w, 1)

    w_copy.wait()
    outer_in = remote(w_mine.at[my_rows], w_mine.at[my_rows], os, orr, outer)
    w_send(0, 0, 1)
    w_send(0, 0, -1)
    w_share(0, 0, 0)

    steps = [(i, j) for i in range(PER) for j in ORDER]
    passed = 0

    def pass_up_to(n):
        nonlocal passed
        while passed < min(n, len(steps)):
            i, j = steps[passed]
            if j != 0:
                x_in[i, j].wait_recv()
                forward(i, j)
            passed += 1

    def attend(i, j):
        scale = scale_ref[PER * x + i] * (1.0 / math.sqrt(HEAD))
        rate = scale * math.log2(math.e)

        scores = lax.dot_general(
            qb[i, :, 128:256], kv[i, j, :, 0:128], NT, preferred_element_type=jnp.float32
        )
        slopes = lax.dot_general(
            qb[i], kv[i, j, :, 0:256], NT, preferred_element_type=jnp.float32
        )
        probs = jnp.exp2(scores * rate)
        weighted = probs * (slopes * scale)
        p_sum = probs[:, 0:128]
        w_sum = weighted[:, 0:128]
        for part in range(1, KEYS // 128):
            p_sum = p_sum + probs[:, part * 128 : (part + 1) * 128]
            w_sum = w_sum + weighted[:, part * 128 : (part + 1) * 128]
        p_mix = jnp.dot(
            probs.astype(jnp.bfloat16), kv[i, j, :, 256:512], preferred_element_type=jnp.float32
        )
        w_mix = jnp.dot(
            weighted.astype(jnp.bfloat16), kv[i, j, :, 256:384], preferred_element_type=jnp.float32
        )
        if j == 0:
            tot[...] = p_sum
            mom[...] = w_sum
            pv[...] = p_mix
            uv[...] = w_mix
        else:
            tot[...] += p_sum
            mom[...] += w_sum
            pv[...] += p_mix
            uv[...] += w_mix

    def finish(i):
        first = x * 256 + i * HEAD if i < 2 else 1024 + x * HEAD
        cols = pl.ds(pl.multiple_of(first, HEAD), HEAD)
        for j in (2, 1, 3, 0):
            rows = pl.ds(j * ROWS, ROWS)
            inv = 1.0 / jnp.sum(tot[rows, :], -1, keepdims=True)
            moment = jnp.sum(mom[rows, :], -1, keepdims=True) * inv
            mixed = pv[rows, 0:128]
            main = (mixed * inv).astype(jnp.bfloat16)
            tangent = ((uv[rows, :] + pv[rows, 128:256] - mixed * moment) * inv).astype(jnp.bfloat16)
            if j == 0:
                att[0:ROWS, cols] = main
                att[ROWS : 2 * ROWS, cols] = tangent
            else:
                ret[i, j - 1, 0:ROWS, :] = main
                ret[i, j - 1, ROWS : 2 * ROWS, :] = tangent
                r_in[i, j] = remote(
                    ret.at[i, j - 1], att.at[:, cols], rs.at[i, j], rr.at[i, j], at_x(NX - j)
                )

    s_copy.wait()
    pass_up_to(AHEAD)
    relay(*steps[0])
    for n, (i, j) in enumerate(steps):
        pass_up_to(n + 1 + AHEAD)
        if n == W_OTHER:
            outer_in.wait_recv()
            w_send(0, 1, 1)
            w_send(0, 1, -1)
            w_share(0, 1, 1)
        for arrival in W_PLAN.get(n, ()):
            w_pass(arrival)
        if n + 1 < len(steps):
            relay(*steps[n + 1])
        if j == 0:
            for other in ORDER[1:]:
                q_in[i, other].wait_recv()
        c_in[i, j].wait_recv()
        d_in[i, j].wait_recv()
        attend(i, j)
        if j == ORDER[-1]:
            finish(i)

    loads[6].wait()
    loads[7].wait()

    def product(half, col, first, depth):
        cols = pl.ds(col, 256)
        rows = [half[pl.ds(k * 384 + first, depth), cols] for k in range(NX)]
        start = 0 if first == 0 else 1024
        return jnp.dot(
            att[:, start : start + NX * depth], jnp.concatenate(rows, 0),
            preferred_element_type=jnp.float32,
        )

    for copy in w_in:
        copy.wait_recv()
    for i in range(PER - 1):
        for j in ORDER[1:]:
            r_in[i, j].wait_recv()
    for n, half in enumerate((w_mine, w_other)):
        for col in range(0, HALF, 256):
            part[n, :, col : col + 256] = product(half, col, 0, 256)
    for j in ORDER[1:]:
        r_in[PER - 1, j].wait_recv()
    for n, (half, offset) in enumerate(((w_mine, c), (w_other, 1 - c))):
        for col in range(0, HALF, 256):
            projected = part[n, :, col : col + 256] + product(half, col, 256, HEAD)
            cols = pl.ds(pl.multiple_of(offset * HALF + col, 256), 256)
            gate, gate_tan = gates[0:1, cols], gates[1:2, cols]
            out_ref[:, cols] = gate * projected[0:ROWS]
            tan_ref[:, cols] = gate_tan * projected[0:ROWS] + gate * projected[ROWS:]
    for copy in sent:
        copy.wait_send()


def attention(q_raw, q_tan, k_raw, k_tan, values, values_tan, w_out, gate, gate_tan, head_scale):
    bf16, f32 = jnp.bfloat16, jnp.float32
    dma = pltpu.SemaphoreType.DMA
    any_spec = pl.BlockSpec(memory_space=pl.ANY)
    return pl.pallas_call(
        body,
        out_shape=[jax.ShapeDtypeStruct((ROWS, HD), f32)] * 2,
        in_specs=[any_spec] * 10,
        out_specs=[pl.BlockSpec(memory_space=pltpu.VMEM)] * 2,
        scratch_shapes=[
            pltpu.VMEM((6, ROWS, HD), bf16),
            pltpu.VMEM((2, HD), f32),
            pltpu.SMEM((HEADS,), f32),
            pltpu.VMEM((PER, NX, KEYS, 512), bf16),
            pltpu.VMEM((PER, NX - 1, ROWS, 512), bf16),
            pltpu.VMEM((PER, KEYS, 256), bf16),
            pltpu.VMEM((PER, NX - 1, ROWS, 256), bf16),
            pltpu.VMEM((KEYS, 256), f32),
            pltpu.VMEM((KEYS, 128), f32),
            pltpu.VMEM((KEYS, 128), f32),
            pltpu.VMEM((KEYS, 128), f32),
            pltpu.VMEM((PER, NX - 1, 2 * ROWS, HEAD), bf16),
            pltpu.VMEM((2 * ROWS, HD), bf16),
            pltpu.VMEM((2, 2 * ROWS, HALF), f32),
            pltpu.VMEM((HD, HALF), bf16),
            pltpu.VMEM((HD, HALF), bf16),
            dma((6,)),
        ]
        + [dma((PER, NX))] * 12
        + [pltpu.SemaphoreType.REGULAR] * 2
        + [dma((2,)), dma, dma, dma, dma]
        + [dma((7,)), dma((7,)), dma((7,)), dma((7,)), dma((16,)), dma((16,))],
        compiler_params=pltpu.CompilerParams(
            collective_id=0, has_side_effects=True, vmem_limit_bytes=48 * 1024 * 1024
        ),
        cost_estimate=pl.CostEstimate(
            flops=7_000_000_000, bytes_accessed=10_000_000, transcendentals=3_200_000
        ),
        name="attention",
    )(q_raw, q_tan, k_raw, k_tan, values, values_tan, w_out, gate, gate_tan, head_scale)


def shards(q_raw, q_tan, k_raw, k_tan, values, values_tan, head_scale, w_out, gate, gate_tan):
    arrays = (q_raw, q_tan, k_raw, k_tan, values, values_tan, w_out, gate, gate_tan, head_scale)
    main, tangent = attention(
        *(pltpu.with_memory_space_constraint(array, pltpu.HBM) for array in arrays)
    )
    return (main.astype(jnp.bfloat16)[None], tangent.astype(jnp.bfloat16)[None])


def solution(mesh):
    rows = P("dp", "blk", None)
    return jax.shard_map(
        shards,
        mesh=mesh,
        in_specs=(rows,) * 6 + (P(), P("dp", None), P("dp", None), P("dp", None)),
        out_specs=(rows, rows),
        check_vma=False,
    )
```

```python
import math

import jax
import jax.numpy as jnp
from jax import lax
from jax.experimental import pallas as pl
from jax.experimental.pallas import tpu as pltpu
from jax.sharding import PartitionSpec as P

HEADS = 12
HEAD = 128
HD = 1536
ROWS = 128
NX = 4
PER = 3
KEYS = 512
DP_ROWS = 96
HALF = 768
MESH = pl.DeviceIdType.MESH
NT = (((1,), (1,)), ((), ()))
ORDER = (0, 1, 3, 2)
AHEAD = 5
W_PLAN = {0: (0,), 1: (1,), 3: (2,), 5: (3,), 7: (4,), 9: (5,), 11: (6,)}

epsilon = 1e-06


def unit_rows(x, dx):
    recip = lax.rsqrt(jnp.mean(x * x, -1, keepdims=True) + epsilon)
    normed = x * recip
    moved = recip * (dx - normed * jnp.mean(normed * dx, -1, keepdims=True))
    return normed.astype(jnp.bfloat16), moved.astype(jnp.bfloat16)


def body(
    q_hbm, qt_hbm, k_hbm, kt_hbm, v_hbm, vt_hbm, w_hbm, gate_hbm, gate_tan_hbm, scale_hbm, out_ref, tan_ref,
    raw, gates, scale_ref, kv, kv_send, qb, q_send, pv, uv, tot, mom, ret, att, part, w_mine, w_other,
    load_sem, xs, xr, qs, qr, ys, yr, cs, cr, ds, dr, rs, rr,
    go_clip, go_w, g_load, s_load, w_load, os, orr, ps, pr, ms, mr, ws, wr,
):
    blk, dp = lax.axis_index("blk"), lax.axis_index("dp")
    y, x, c = blk // 8, (blk // 2) % NX, blk % 2
    z, yh = dp // 2, dp % 2

    def at_x(j):
        return {"dp": dp, "blk": y * 8 + ((x + j) % NX) * 2 + c}

    y_peer = {"dp": dp, "blk": (1 - y) * 8 + x * 2 + c}
    c_peer = {"dp": dp, "blk": y * 8 + x * 2 + (1 - c)}
    outer = {"dp": z * 2 + (1 - yh), "blk": (1 - y) * 8 + x * 2 + c}
    z_up = {"dp": ((z + 1) % 8) * 2 + yh, "blk": blk}
    z_down = {"dp": ((z + 7) % 8) * 2 + yh, "blk": blk}

    barrier = pltpu.get_barrier_semaphore()

    def greet(peer):
        pl.semaphore_signal(barrier, inc=1, device_id=peer, device_id_type=MESH)

    for j in range(1, NX):
        greet({"dp": dp, "blk": y * 8 + ((x + j) % NX) * 2})
    greet({"dp": dp, "blk": (1 - y) * 8 + x * 2})
    pl.when(c == 1)(lambda: greet({"dp": dp, "blk": y * 8 + x * 2}))
    greet({"dp": z * 2 + (1 - yh), "blk": (1 - y) * 8 + x * 2 + 1})
    greet({"dp": ((z + 1) % 8) * 2 + yh, "blk": y * 8 + x * 2 + 1})
    greet({"dp": ((z + 7) % 8) * 2 + yh, "blk": y * 8 + x * 2 + 1})
    loads = []
    for n, src in enumerate((k_hbm, kt_hbm, v_hbm, vt_hbm, q_hbm, qt_hbm)):
        copy = pltpu.make_async_copy(src.at[0], raw.at[n], load_sem.at[n])
        copy.start()
        loads.append(copy)
    my_rows = pl.ds(pl.multiple_of(dp * DP_ROWS, DP_ROWS), DP_ROWS)
    my_cols = pl.ds(pl.multiple_of(c * HALF, HALF), HALF)
    w_copy = pltpu.make_async_copy(w_hbm.at[:, my_cols], w_mine.at[my_rows], w_load)
    w_copy.start()
    for n, src in enumerate((gate_hbm, gate_tan_hbm)):
        copy = pltpu.make_async_copy(src, gates.at[pl.ds(n, 1)], g_load.at[n])
        copy.start()
        loads.append(copy)
    s_copy = pltpu.make_async_copy(scale_hbm, scale_ref, s_load)
    s_copy.start()

    @pl.when(c == 0)
    def _():
        pl.semaphore_wait(barrier, 9)
        pl.semaphore_signal(go_clip, inc=1, device_id=c_peer, device_id_type=MESH)

    @pl.when(c == 1)
    def _():
        pl.semaphore_wait(go_clip, 1)


    sent = []

    def remote(src, dst, send_sem, recv_sem, peer):
        copy = pltpu.make_async_remote_copy(
            src_ref=src, dst_ref=dst, send_sem=send_sem, recv_sem=recv_sem,
            device_id=peer, device_id_type=MESH,
        )
        copy.start()
        sent.append(copy)
        return copy

    x_in, q_in, y_in, c_in, d_in, r_in = {}, {}, {}, {}, {}, {}

    def forward(i, j):
        own = kv.at[i, j, pl.ds(0, ROWS)]
        y_in[i, j] = remote(own, kv.at[i, j, pl.ds(ROWS, ROWS)], ys.at[i, j], yr.at[i, j], y_peer)
        c_in[i, j] = remote(own, kv.at[i, j, pl.ds(2 * ROWS, ROWS)], cs.at[i, j], cr.at[i, j], c_peer)

    def relay(i, j):
        y_in[i, j].wait_recv()
        d_in[i, j] = remote(
            kv.at[i, j, pl.ds(ROWS, ROWS)], kv.at[i, j, pl.ds(3 * ROWS, ROWS)],
            ds.at[i, j], dr.at[i, j], c_peer,
        )

    def columns(i, j):
        head = PER * ((x + j) % NX) + i
        return pl.ds(pl.multiple_of(head * HEAD, HEAD), HEAD)

    def send_keys(i, j):
        cols = columns(i, j)
        normed, moved = unit_rows(
            raw[0, :, cols].astype(jnp.float32), raw[1, :, cols].astype(jnp.float32)
        )
        dst = kv.at[i, 0, pl.ds(0, ROWS)] if j == 0 else kv_send.at[i, j - 1]
        dst[:, 0:128] = normed
        dst[:, 128:256] = moved
        dst[:, 256:384] = raw[2, :, cols]
        dst[:, 384:512] = raw[3, :, cols]
        if j == 0:
            forward(i, 0)
        else:
            x_in[i, j] = remote(
                dst, kv.at[i, j, pl.ds(0, ROWS)], xs.at[i, j], xr.at[i, j], at_x(j)
            )

    def send_queries(i, j):
        cols = columns(i, j)
        normed, moved = unit_rows(
            raw[4, :, cols].astype(jnp.float32), raw[5, :, cols].astype(jnp.float32)
        )
        dst = qb.at[i, pl.ds(0, ROWS)] if j == 0 else q_send.at[i, j - 1]
        dst[:, 0:128] = moved
        dst[:, 128:256] = normed
        if j != 0:
            q_in[i, j] = remote(
                dst, qb.at[i, pl.ds(j * ROWS, ROWS)], qs.at[i, j], qr.at[i, j], at_x(j)
            )

    def piece(distance, other):
        row = (((z + distance + 8) % 8) * 2 + (1 - yh if other else yh)) * DP_ROWS
        return w_mine.at[pl.ds(pl.multiple_of(row, DP_ROWS), DP_ROWS)], w_other.at[
            pl.ds(pl.multiple_of(row, DP_ROWS), DP_ROWS)
        ]

    up_in, down_in, w_in = {}, {}, []

    def w_send(distance, other, going):
        if going > 0:
            n = 2 * distance + other
            here = piece(-distance, other)[0]
            up_in[n] = remote(here, here, ps.at[n], pr.at[n], z_up)
        else:
            n = 2 * distance + other if distance < 3 else 6
            here = piece(distance, other)[0]
            down_in[n] = remote(here, here, ms.at[n], mr.at[n], z_down)

    def w_share(distance, other, n):
        here, there = piece(distance, other)
        w_in.append(remote(here, there, ws.at[n], wr.at[n], c_peer))

    def w_pass(n):
        up_in[n].wait_recv()
        down_in[n].wait_recv()
        distance, other = n // 2 + 1, n % 2
        if n < 5:
            w_send(distance, other, 1)
        if n < 4:
            w_send(distance, other, -1)
        if n == 5:
            w_send(3, 1, -1)
        w_share(-distance, other, 2 + n)
        w_share(distance, other if n < 6 else 1, 9 + n)

    for n in range(4):
        loads[n].wait()
    for j in ORDER:
        send_keys(0, j)
    loads[4].wait()
    loads[5].wait()
    for j in ORDER:
        send_queries(0, j)

    for i in range(1, PER):
        send_keys(i, 0)

    @pl.when(c == 1)
    def _():
        pl.semaphore_wait(barrier, 6)
        pl.semaphore_signal(go_w, inc=1, device_id=c_peer, device_id_type=MESH)

    @pl.when(c == 0)
    def _():
        pl.semaphore_wait(go_w, 1)

    w_copy.wait()
    outer_in = remote(w_mine.at[my_rows], w_mine.at[my_rows], os, orr, outer)
    w_send(0, 0, 1)
    w_send(0, 0, -1)
    w_share(0, 0, 0)
    for i in range(1, PER):
        for j in ORDER[1:]:
            send_keys(i, j)
        for j in ORDER:
            send_queries(i, j)

    steps = [(i, j) for i in range(PER) for j in ORDER]
    passed = 0

    def pass_up_to(n):
        nonlocal passed
        while passed < min(n, len(steps)):
            i, j = steps[passed]
            if j != 0:
                x_in[i, j].wait_recv()
                forward(i, j)
            passed += 1

    def attend(i, j):
        scale = scale_ref[PER * x + i] * (1.0 / math.sqrt(HEAD))
        rate = scale * math.log2(math.e)

        scores = lax.dot_general(
            qb[i, :, 128:256], kv[i, j, :, 0:128], NT, preferred_element_type=jnp.float32
        )
        slopes = lax.dot_general(
            qb[i], kv[i, j, :, 0:256], NT, preferred_element_type=jnp.float32
        )
        probs = jnp.exp2(scores * rate)
        weighted = probs * (slopes * scale)
        p_sum = probs[:, 0:128]
        w_sum = weighted[:, 0:128]
        for part in range(1, KEYS // 128):
            p_sum = p_sum + probs[:, part * 128 : (part + 1) * 128]
            w_sum = w_sum + weighted[:, part * 128 : (part + 1) * 128]
        p_mix = jnp.dot(
            probs.astype(jnp.bfloat16), kv[i, j, :, 256:512], preferred_element_type=jnp.float32
        )
        w_mix = jnp.dot(
            weighted.astype(jnp.bfloat16), kv[i, j, :, 256:384], preferred_element_type=jnp.float32
        )
        if j == 0:
            tot[...] = p_sum
            mom[...] = w_sum
            pv[...] = p_mix
            uv[...] = w_mix
        else:
            tot[...] += p_sum
            mom[...] += w_sum
            pv[...] += p_mix
            uv[...] += w_mix

    def finish(i):
        for j in (2, 1, 3, 0):
            rows = pl.ds(j * ROWS, ROWS)
            inv = 1.0 / jnp.sum(tot[rows, :], -1, keepdims=True)
            moment = jnp.sum(mom[rows, :], -1, keepdims=True) * inv
            mixed = pv[rows, 0:128]
            main = (mixed * inv).astype(jnp.bfloat16)
            tangent = ((uv[rows, :] + pv[rows, 128:256] - mixed * moment) * inv).astype(jnp.bfloat16)
            if j == 0:
                att[i, x, 0:ROWS, :] = main
                att[i, x, ROWS : 2 * ROWS, :] = tangent
            else:
                ret[i, j - 1, 0:ROWS, :] = main
                ret[i, j - 1, ROWS : 2 * ROWS, :] = tangent
                r_in[i, j] = remote(
                    ret.at[i, j - 1], att.at[i, x], rs.at[i, j], rr.at[i, j], at_x(NX - j)
                )

    s_copy.wait()
    outer_in.wait_recv()
    w_send(0, 1, 1)
    w_send(0, 1, -1)
    w_share(0, 1, 1)
    pass_up_to(AHEAD)
    relay(*steps[0])
    for n, (i, j) in enumerate(steps):
        pass_up_to(n + 1 + AHEAD)
        for arrival in W_PLAN.get(n, ()):
            w_pass(arrival)
        if n + 1 < len(steps):
            relay(*steps[n + 1])
        if j == 0:
            for other in ORDER[1:]:
                q_in[i, other].wait_recv()
        c_in[i, j].wait_recv()
        d_in[i, j].wait_recv()
        attend(i, j)
        if j == ORDER[-1]:
            finish(i)

    loads[6].wait()
    loads[7].wait()

    def product(half, col, heads):
        pairs = [(i, k) for k in range(NX) for i in heads]
        rows = [half[pl.ds((PER * k + i) * HEAD, HEAD), pl.ds(col, 256)] for i, k in pairs]
        return jnp.dot(
            jnp.concatenate([att[i, k] for i, k in pairs], 1), jnp.concatenate(rows, 0),
            preferred_element_type=jnp.float32,
        )

    for copy in w_in:
        copy.wait_recv()
    for i in range(PER - 1):
        for j in ORDER[1:]:
            r_in[i, j].wait_recv()
    for n, half in enumerate((w_mine, w_other)):
        for col in range(0, HALF, 256):
            part[n, :, col : col + 256] = product(half, col, (0, 1))
    for j in ORDER[1:]:
        r_in[PER - 1, j].wait_recv()
    for n, (half, offset) in enumerate(((w_mine, c), (w_other, 1 - c))):
        for col in range(0, HALF, 256):
            projected = part[n, :, col : col + 256] + product(half, col, (2,))
            cols = pl.ds(pl.multiple_of(offset * HALF + col, 256), 256)
            gate, gate_tan = gates[0:1, cols], gates[1:2, cols]
            out_ref[:, cols] = gate * projected[0:ROWS]
            tan_ref[:, cols] = gate_tan * projected[0:ROWS] + gate * projected[ROWS:]
    for copy in sent:
        copy.wait_send()


def attention(q_raw, q_tan, k_raw, k_tan, values, values_tan, w_out, gate, gate_tan, head_scale):
    bf16, f32 = jnp.bfloat16, jnp.float32
    dma = pltpu.SemaphoreType.DMA
    any_spec = pl.BlockSpec(memory_space=pl.ANY)
    return pl.pallas_call(
        body,
        out_shape=[jax.ShapeDtypeStruct((ROWS, HD), f32)] * 2,
        in_specs=[any_spec] * 10,
        out_specs=[pl.BlockSpec(memory_space=pltpu.VMEM)] * 2,
        scratch_shapes=[
            pltpu.VMEM((6, ROWS, HD), bf16),
            pltpu.VMEM((2, HD), f32),
            pltpu.SMEM((HEADS,), f32),
            pltpu.VMEM((PER, NX, KEYS, 512), bf16),
            pltpu.VMEM((PER, NX - 1, ROWS, 512), bf16),
            pltpu.VMEM((PER, KEYS, 256), bf16),
            pltpu.VMEM((PER, NX - 1, ROWS, 256), bf16),
            pltpu.VMEM((KEYS, 256), f32),
            pltpu.VMEM((KEYS, 128), f32),
            pltpu.VMEM((KEYS, 128), f32),
            pltpu.VMEM((KEYS, 128), f32),
            pltpu.VMEM((PER, NX - 1, 2 * ROWS, HEAD), bf16),
            pltpu.VMEM((PER, NX, 2 * ROWS, HEAD), bf16),
            pltpu.VMEM((2, 2 * ROWS, HALF), f32),
            pltpu.VMEM((HD, HALF), bf16),
            pltpu.VMEM((HD, HALF), bf16),
            dma((6,)),
        ]
        + [dma((PER, NX))] * 12
        + [pltpu.SemaphoreType.REGULAR] * 2
        + [dma((2,)), dma, dma, dma, dma]
        + [dma((7,)), dma((7,)), dma((7,)), dma((7,)), dma((16,)), dma((16,))],
        compiler_params=pltpu.CompilerParams(
            collective_id=0, has_side_effects=True, vmem_limit_bytes=48 * 1024 * 1024
        ),
        cost_estimate=pl.CostEstimate(
            flops=7_000_000_000, bytes_accessed=10_000_000, transcendentals=3_200_000
        ),
        name="attention",
    )(q_raw, q_tan, k_raw, k_tan, values, values_tan, w_out, gate, gate_tan, head_scale)


def shards(q_raw, q_tan, k_raw, k_tan, values, values_tan, head_scale, w_out, gate, gate_tan):
    arrays = (q_raw, q_tan, k_raw, k_tan, values, values_tan, w_out, gate, gate_tan, head_scale)
    main, tangent = attention(
        *(pltpu.with_memory_space_constraint(array, pltpu.HBM) for array in arrays)
    )
    return (main.astype(jnp.bfloat16)[None], tangent.astype(jnp.bfloat16)[None])


def solution(mesh):
    rows = P("dp", "blk", None)
    return jax.shard_map(
        shards,
        mesh=mesh,
        in_specs=(rows,) * 6 + (P(), P("dp", None), P("dp", None), P("dp", None)),
        out_specs=(rows, rows),
        check_vma=False,
    )
```

```python
import math

import jax
import jax.numpy as jnp
from jax import lax
from jax.experimental import pallas as pl
from jax.experimental.pallas import tpu as pltpu
from jax.sharding import PartitionSpec as P

HEADS = 12
HEAD = 128
HD = 1536
ROWS = 128
NX = 4
PER = 3
KEYS = 512
DP_ROWS = 96
HALF = 768
MESH = pl.DeviceIdType.MESH
NT = (((1,), (1,)), ((), ()))
ORDER = (0, 1, 3, 2)
AHEAD = 5
OWN, MATE, ACROSS, DIAGONAL = range(4)
SPLIT = 96
W_PLAN = {0: (0,), 1: (1,), 3: (2,), 5: (3,), 7: (4,), 9: (5,), 11: (6,)}

epsilon = 1e-06


def unit_rows(x, dx):
    recip = lax.rsqrt(jnp.mean(x * x, -1, keepdims=True) + epsilon)
    normed = x * recip
    moved = recip * (dx - normed * jnp.mean(normed * dx, -1, keepdims=True))
    return normed.astype(jnp.bfloat16), moved.astype(jnp.bfloat16)


def body(
    q_hbm, qt_hbm, k_hbm, kt_hbm, v_hbm, vt_hbm, w_hbm, gate_hbm, gate_tan_hbm, scale_hbm, out_ref, tan_ref,
    raw, gates, scale_ref, kv, kv_send, qb, q_send, pv, uv, tot, mom, ret, att, part, w_mine, w_other,
    load_sem, xs, xr, qs, qr, ys, yr, cs, cr, ds, dr, rs, rr,
    fs, fr, go_clip, go_w, g_load, s_load, w_load, os, orr, ps, pr, ms, mr, ws, wr,
):
    blk, dp = lax.axis_index("blk"), lax.axis_index("dp")
    y, x, c = blk // 8, (blk // 2) % NX, blk % 2
    z, yh = dp // 2, dp % 2

    def at_x(j):
        return {"dp": dp, "blk": y * 8 + ((x + j) % NX) * 2 + c}

    y_peer = {"dp": dp, "blk": (1 - y) * 8 + x * 2 + c}
    c_peer = {"dp": dp, "blk": y * 8 + x * 2 + (1 - c)}
    diagonal = {"dp": dp, "blk": (1 - y) * 8 + x * 2 + (1 - c)}
    outer = {"dp": z * 2 + (1 - yh), "blk": (1 - y) * 8 + x * 2 + c}
    z_up = {"dp": ((z + 1) % 8) * 2 + yh, "blk": blk}
    z_down = {"dp": ((z + 7) % 8) * 2 + yh, "blk": blk}

    barrier = pltpu.get_barrier_semaphore()

    def greet(peer):
        pl.semaphore_signal(barrier, inc=1, device_id=peer, device_id_type=MESH)

    for j in range(1, NX):
        greet({"dp": dp, "blk": y * 8 + ((x + j) % NX) * 2})
    greet({"dp": dp, "blk": (1 - y) * 8 + x * 2})
    pl.when(c == 1)(lambda: greet({"dp": dp, "blk": y * 8 + x * 2}))
    greet({"dp": z * 2 + (1 - yh), "blk": (1 - y) * 8 + x * 2 + 1})
    greet({"dp": ((z + 1) % 8) * 2 + yh, "blk": y * 8 + x * 2 + 1})
    greet({"dp": ((z + 7) % 8) * 2 + yh, "blk": y * 8 + x * 2 + 1})
    loads = []
    for n, src in enumerate((k_hbm, kt_hbm, v_hbm, vt_hbm, q_hbm, qt_hbm)):
        copy = pltpu.make_async_copy(src.at[0], raw.at[n], load_sem.at[n])
        copy.start()
        loads.append(copy)
    my_rows = pl.ds(pl.multiple_of(dp * DP_ROWS, DP_ROWS), DP_ROWS)
    my_cols = pl.ds(pl.multiple_of(c * HALF, HALF), HALF)
    w_copy = pltpu.make_async_copy(w_hbm.at[:, my_cols], w_mine.at[my_rows], w_load)
    w_copy.start()
    for n, src in enumerate((gate_hbm, gate_tan_hbm)):
        copy = pltpu.make_async_copy(src, gates.at[pl.ds(n, 1)], g_load.at[n])
        copy.start()
        loads.append(copy)
    s_copy = pltpu.make_async_copy(scale_hbm, scale_ref, s_load)
    s_copy.start()

    @pl.when(c == 0)
    def _():
        pl.semaphore_wait(barrier, 9)
        pl.semaphore_signal(go_clip, inc=1, device_id=c_peer, device_id_type=MESH)

    @pl.when(c == 1)
    def _():
        pl.semaphore_wait(go_clip, 1)


    sent = []

    def remote(src, dst, send_sem, recv_sem, peer):
        copy = pltpu.make_async_remote_copy(
            src_ref=src, dst_ref=dst, send_sem=send_sem, recv_sem=recv_sem,
            device_id=peer, device_id_type=MESH,
        )
        copy.start()
        sent.append(copy)
        return copy

    x_in, q_in, y_in, c_in, d_in, r_in = {}, {}, {}, {}, {}, {}

    last = (PER - 1, ORDER[-1])
    tails = []

    def keys_from(i, j, place, start=0, size=ROWS):
        return kv.at[i, j, pl.ds(place * ROWS + start, size)]

    def forward(i, j):
        own = keys_from(i, j, OWN)
        size = ROWS if (i, j) != last else SPLIT
        y_in[i, j] = remote(
            keys_from(i, j, OWN, 0, size), keys_from(i, j, ACROSS, 0, size),
            ys.at[i, j], yr.at[i, j], y_peer,
        )
        if (i, j) == last:
            for n, (place, peer) in enumerate(((ACROSS, y_peer), (DIAGONAL, diagonal))):
                tails.append(
                    remote(
                        keys_from(i, j, OWN, SPLIT, ROWS - SPLIT),
                        keys_from(i, j, place, SPLIT, ROWS - SPLIT), fs.at[n], fr.at[n], peer,
                    )
                )
        c_in[i, j] = remote(own, keys_from(i, j, MATE), cs.at[i, j], cr.at[i, j], c_peer)

    def relay(i, j):
        size = ROWS if (i, j) != last else SPLIT
        y_in[i, j].wait_recv()
        d_in[i, j] = remote(
            keys_from(i, j, ACROSS, 0, size), keys_from(i, j, DIAGONAL, 0, size),
            ds.at[i, j], dr.at[i, j], c_peer,
        )

    def columns(i, j):
        head = PER * ((x + j) % NX) + i
        return pl.ds(pl.multiple_of(head * HEAD, HEAD), HEAD)

    def send_keys(i, j):
        cols = columns(i, j)
        normed, moved = unit_rows(
            raw[0, :, cols].astype(jnp.float32), raw[1, :, cols].astype(jnp.float32)
        )
        dst = kv.at[i, 0, pl.ds(0, ROWS)] if j == 0 else kv_send.at[i, j - 1]
        dst[:, 0:128] = normed
        dst[:, 128:256] = moved
        dst[:, 256:384] = raw[2, :, cols]
        dst[:, 384:512] = raw[3, :, cols]
        if j == 0:
            forward(i, 0)
        else:
            x_in[i, j] = remote(
                dst, kv.at[i, j, pl.ds(0, ROWS)], xs.at[i, j], xr.at[i, j], at_x(j)
            )

    def send_queries(i, j):
        cols = columns(i, j)
        normed, moved = unit_rows(
            raw[4, :, cols].astype(jnp.float32), raw[5, :, cols].astype(jnp.float32)
        )
        dst = qb.at[i, pl.ds(0, ROWS)] if j == 0 else q_send.at[i, j - 1]
        dst[:, 0:128] = moved
        dst[:, 128:256] = normed
        if j != 0:
            q_in[i, j] = remote(
                dst, qb.at[i, pl.ds(j * ROWS, ROWS)], qs.at[i, j], qr.at[i, j], at_x(j)
            )

    def piece(distance, other):
        row = (((z + distance + 8) % 8) * 2 + (1 - yh if other else yh)) * DP_ROWS
        return w_mine.at[pl.ds(pl.multiple_of(row, DP_ROWS), DP_ROWS)], w_other.at[
            pl.ds(pl.multiple_of(row, DP_ROWS), DP_ROWS)
        ]

    up_in, down_in, w_in = {}, {}, []

    def w_send(distance, other, going):
        if going > 0:
            n = 2 * distance + other
            here = piece(-distance, other)[0]
            up_in[n] = remote(here, here, ps.at[n], pr.at[n], z_up)
        else:
            n = 2 * distance + other if distance < 3 else 6
            here = piece(distance, other)[0]
            down_in[n] = remote(here, here, ms.at[n], mr.at[n], z_down)

    def w_share(distance, other, n):
        here, there = piece(distance, other)
        w_in.append(remote(here, there, ws.at[n], wr.at[n], c_peer))

    def w_pass(n):
        up_in[n].wait_recv()
        down_in[n].wait_recv()
        distance, other = n // 2 + 1, n % 2
        if n < 5:
            w_send(distance, other, 1)
        if n < 4:
            w_send(distance, other, -1)
        if n == 5:
            w_send(3, 1, -1)
        w_share(-distance, other, 2 + n)
        w_share(distance, other if n < 6 else 1, 9 + n)

    for n in range(4):
        loads[n].wait()
    for j in ORDER:
        send_keys(0, j)
    loads[4].wait()
    loads[5].wait()
    for j in ORDER:
        send_queries(0, j)

    for i in range(1, PER):
        send_keys(i, 0)

    @pl.when(c == 1)
    def _():
        pl.semaphore_wait(barrier, 6)
        pl.semaphore_signal(go_w, inc=1, device_id=c_peer, device_id_type=MESH)

    @pl.when(c == 0)
    def _():
        pl.semaphore_wait(go_w, 1)

    w_copy.wait()
    outer_in = remote(w_mine.at[my_rows], w_mine.at[my_rows], os, orr, outer)
    w_send(0, 0, 1)
    w_send(0, 0, -1)
    w_share(0, 0, 0)
    for i in range(1, PER):
        for j in ORDER[1:]:
            send_keys(i, j)
        for j in ORDER:
            send_queries(i, j)

    steps = [(i, j) for i in range(PER) for j in ORDER]
    passed = 0

    def pass_up_to(n):
        nonlocal passed
        while passed < min(n, len(steps)):
            i, j = steps[passed]
            if j != 0:
                x_in[i, j].wait_recv()
                forward(i, j)
            passed += 1

    def attend(i, j, first, count, start=0, size=KEYS):
        keys, rows = pl.ds(first, count), pl.ds(start, size)
        scale = scale_ref[PER * x + i] * (1.0 / math.sqrt(HEAD))
        rate = scale * math.log2(math.e)

        scores = lax.dot_general(
            qb[i, rows, 128:256], kv[i, j, keys, 0:128], NT, preferred_element_type=jnp.float32
        )
        slopes = lax.dot_general(
            qb[i, rows, :], kv[i, j, keys, 0:256], NT, preferred_element_type=jnp.float32
        )
        probs = jnp.exp2(scores * rate)
        weighted = probs * (slopes * scale)
        p_sum = probs[:, 0:128]
        w_sum = weighted[:, 0:128]
        for part in range(1, count // 128):
            p_sum = p_sum + probs[:, part * 128 : (part + 1) * 128]
            w_sum = w_sum + weighted[:, part * 128 : (part + 1) * 128]
        p_mix = jnp.dot(
            probs.astype(jnp.bfloat16), kv[i, j, keys, 256:512], preferred_element_type=jnp.float32
        )
        w_mix = jnp.dot(
            weighted.astype(jnp.bfloat16), kv[i, j, keys, 256:384], preferred_element_type=jnp.float32
        )
        if j == 0:
            tot[rows, :] = p_sum
            mom[rows, :] = w_sum
            pv[rows, :] = p_mix
            uv[rows, :] = w_mix
        else:
            tot[rows, :] += p_sum
            mom[rows, :] += w_sum
            pv[rows, :] += p_mix
            uv[rows, :] += w_mix

    def finish(i, parts=(2, 1, 3, 0)):
        for j in parts:
            rows = pl.ds(j * ROWS, ROWS)
            inv = 1.0 / jnp.sum(tot[rows, :], -1, keepdims=True)
            moment = jnp.sum(mom[rows, :], -1, keepdims=True) * inv
            mixed = pv[rows, 0:128]
            main = (mixed * inv).astype(jnp.bfloat16)
            tangent = ((uv[rows, :] + pv[rows, 128:256] - mixed * moment) * inv).astype(jnp.bfloat16)
            if j == 0:
                att[i, x, 0:ROWS, :] = main
                att[i, x, ROWS : 2 * ROWS, :] = tangent
            else:
                ret[i, j - 1, 0:ROWS, :] = main
                ret[i, j - 1, ROWS : 2 * ROWS, :] = tangent
                r_in[i, j] = remote(
                    ret.at[i, j - 1], att.at[i, x], rs.at[i, j], rr.at[i, j], at_x(NX - j)
                )

    s_copy.wait()
    outer_in.wait_recv()
    w_send(0, 1, 1)
    w_send(0, 1, -1)
    w_share(0, 1, 1)
    pass_up_to(AHEAD)
    relay(*steps[0])
    for n, (i, j) in enumerate(steps):
        pass_up_to(n + 1 + AHEAD)
        for arrival in W_PLAN.get(n, ()):
            w_pass(arrival)
        if n + 1 < len(steps):
            relay(*steps[n + 1])
        if j == 0:
            for other in ORDER[1:]:
                q_in[i, other].wait_recv()
        c_in[i, j].wait_recv()
        if (i, j) == last:
            attend(i, j, 0, KEYS // 2)
            d_in[i, j].wait_recv()
            for copy in tails:
                copy.wait_recv()
            for parts in ((2, 3), (1, 0)):
                attend(i, j, KEYS // 2, KEYS // 2, min(parts) * ROWS, KEYS // 2)
                finish(i, parts)
        else:
            d_in[i, j].wait_recv()
            attend(i, j, 0, KEYS)
        if j == ORDER[-1] and i < PER - 1:
            finish(i)

    loads[6].wait()
    loads[7].wait()

    def product(half, col, heads):
        pairs = [(i, k) for k in range(NX) for i in heads]
        rows = [half[pl.ds((PER * k + i) * HEAD, HEAD), pl.ds(col, 256)] for i, k in pairs]
        return jnp.dot(
            jnp.concatenate([att[i, k] for i, k in pairs], 1), jnp.concatenate(rows, 0),
            preferred_element_type=jnp.float32,
        )

    for copy in w_in:
        copy.wait_recv()
    for i in range(PER - 1):
        for j in ORDER[1:]:
            r_in[i, j].wait_recv()
    for n, half in enumerate((w_mine, w_other)):
        for col in range(0, HALF, 256):
            part[n, :, col : col + 256] = product(half, col, (0, 1))
    for j in ORDER[1:]:
        r_in[PER - 1, j].wait_recv()
    for n, (half, offset) in enumerate(((w_mine, c), (w_other, 1 - c))):
        for col in range(0, HALF, 256):
            projected = part[n, :, col : col + 256] + product(half, col, (2,))
            cols = pl.ds(pl.multiple_of(offset * HALF + col, 256), 256)
            gate, gate_tan = gates[0:1, cols], gates[1:2, cols]
            out_ref[:, cols] = gate * projected[0:ROWS]
            tan_ref[:, cols] = gate_tan * projected[0:ROWS] + gate * projected[ROWS:]
    for copy in sent:
        copy.wait_send()


def attention(q_raw, q_tan, k_raw, k_tan, values, values_tan, w_out, gate, gate_tan, head_scale):
    bf16, f32 = jnp.bfloat16, jnp.float32
    dma = pltpu.SemaphoreType.DMA
    any_spec = pl.BlockSpec(memory_space=pl.ANY)
    return pl.pallas_call(
        body,
        out_shape=[jax.ShapeDtypeStruct((ROWS, HD), f32)] * 2,
        in_specs=[any_spec] * 10,
        out_specs=[pl.BlockSpec(memory_space=pltpu.VMEM)] * 2,
        scratch_shapes=[
            pltpu.VMEM((6, ROWS, HD), bf16),
            pltpu.VMEM((2, HD), f32),
            pltpu.SMEM((HEADS,), f32),
            pltpu.VMEM((PER, NX, KEYS, 512), bf16),
            pltpu.VMEM((PER, NX - 1, ROWS, 512), bf16),
            pltpu.VMEM((PER, KEYS, 256), bf16),
            pltpu.VMEM((PER, NX - 1, ROWS, 256), bf16),
            pltpu.VMEM((KEYS, 256), f32),
            pltpu.VMEM((KEYS, 128), f32),
            pltpu.VMEM((KEYS, 128), f32),
            pltpu.VMEM((KEYS, 128), f32),
            pltpu.VMEM((PER, NX - 1, 2 * ROWS, HEAD), bf16),
            pltpu.VMEM((PER, NX, 2 * ROWS, HEAD), bf16),
            pltpu.VMEM((2, 2 * ROWS, HALF), f32),
            pltpu.VMEM((HD, HALF), bf16),
            pltpu.VMEM((HD, HALF), bf16),
            dma((6,)),
        ]
        + [dma((PER, NX))] * 12
        + [dma((2,)), dma((2,))]
        + [pltpu.SemaphoreType.REGULAR] * 2
        + [dma((2,)), dma, dma, dma, dma]
        + [dma((7,)), dma((7,)), dma((7,)), dma((7,)), dma((16,)), dma((16,))],
        compiler_params=pltpu.CompilerParams(
            collective_id=0, has_side_effects=True, vmem_limit_bytes=48 * 1024 * 1024
        ),
        cost_estimate=pl.CostEstimate(
            flops=7_000_000_000, bytes_accessed=10_000_000, transcendentals=3_200_000
        ),
        name="attention",
    )(q_raw, q_tan, k_raw, k_tan, values, values_tan, w_out, gate, gate_tan, head_scale)


def shards(q_raw, q_tan, k_raw, k_tan, values, values_tan, head_scale, w_out, gate, gate_tan):
    arrays = (q_raw, q_tan, k_raw, k_tan, values, values_tan, w_out, gate, gate_tan, head_scale)
    main, tangent = attention(
        *(pltpu.with_memory_space_constraint(array, pltpu.HBM) for array in arrays)
    )
    return (main.astype(jnp.bfloat16)[None], tangent.astype(jnp.bfloat16)[None])


def solution(mesh):
    rows = P("dp", "blk", None)
    return jax.shard_map(
        shards,
        mesh=mesh,
        in_specs=(rows,) * 6 + (P(), P("dp", None), P("dp", None), P("dp", None)),
        out_specs=(rows, rows),
        check_vma=False,
    )
```

```python
import math

import jax
import jax.numpy as jnp
from jax import lax
from jax.experimental import pallas as pl
from jax.experimental.pallas import tpu as pltpu
from jax.sharding import PartitionSpec as P

HEADS = 12
HEAD = 128
HD = 1536
ROWS = 128
NX = 4
PER = 3
KEYS = 512
DP_ROWS = 96
HALF = 768
MESH = pl.DeviceIdType.MESH
NT = (((1,), (1,)), ((), ()))
ORDER = (0, 1, 3, 2)
AHEAD = 5
OWN, MATE, ACROSS, DIAGONAL = range(4)
SPLIT = 96
W_PLAN = {0: (0,), 1: (1,), 3: (2,), 5: (3,), 7: (4,), 9: (5,)}

epsilon = 1e-06


def unit_rows(x, dx):
    recip = lax.rsqrt(jnp.mean(x * x, -1, keepdims=True) + epsilon)
    normed = x * recip
    moved = recip * (dx - normed * jnp.mean(normed * dx, -1, keepdims=True))
    return normed.astype(jnp.bfloat16), moved.astype(jnp.bfloat16)


def body(
    q_hbm, qt_hbm, k_hbm, kt_hbm, v_hbm, vt_hbm, w_hbm, gate_hbm, gate_tan_hbm, scale_hbm, out_ref, tan_ref,
    raw, gates, scale_ref, kv, kv_send, qb, q_send, pv, uv, tot, mom, ret, att, part, w_mine, w_other,
    load_sem, xs, xr, qs, qr, ys, yr, cs, cr, ds, dr, rs, rr,
    fs, fr, go_clip, go_w, g_load, s_load, w_load, os, orr, ps, pr, ms, mr, ws, wr,
):
    blk, dp = lax.axis_index("blk"), lax.axis_index("dp")
    y, x, c = blk // 8, (blk // 2) % NX, blk % 2
    z, yh = dp // 2, dp % 2

    def at_x(j):
        return {"dp": dp, "blk": y * 8 + ((x + j) % NX) * 2 + c}

    y_peer = {"dp": dp, "blk": (1 - y) * 8 + x * 2 + c}
    c_peer = {"dp": dp, "blk": y * 8 + x * 2 + (1 - c)}
    diagonal = {"dp": dp, "blk": (1 - y) * 8 + x * 2 + (1 - c)}
    outer = {"dp": z * 2 + (1 - yh), "blk": (1 - y) * 8 + x * 2 + c}
    z_up = {"dp": ((z + 1) % 8) * 2 + yh, "blk": blk}
    z_down = {"dp": ((z + 7) % 8) * 2 + yh, "blk": blk}

    barrier = pltpu.get_barrier_semaphore()

    def greet(peer):
        pl.semaphore_signal(barrier, inc=1, device_id=peer, device_id_type=MESH)

    for j in range(1, NX):
        greet({"dp": dp, "blk": y * 8 + ((x + j) % NX) * 2})
    greet({"dp": dp, "blk": (1 - y) * 8 + x * 2})
    pl.when(c == 1)(lambda: greet({"dp": dp, "blk": y * 8 + x * 2}))
    greet({"dp": z * 2 + (1 - yh), "blk": (1 - y) * 8 + x * 2 + 1})
    greet({"dp": ((z + 1) % 8) * 2 + yh, "blk": y * 8 + x * 2 + 1})
    greet({"dp": ((z + 7) % 8) * 2 + yh, "blk": y * 8 + x * 2 + 1})
    loads = []
    for n, src in enumerate((k_hbm, kt_hbm, v_hbm, vt_hbm, q_hbm, qt_hbm)):
        copy = pltpu.make_async_copy(src.at[0], raw.at[n], load_sem.at[n])
        copy.start()
        loads.append(copy)
    my_rows = pl.ds(pl.multiple_of(dp * DP_ROWS, DP_ROWS), DP_ROWS)
    my_cols = pl.ds(pl.multiple_of(c * HALF, HALF), HALF)
    w_copy = pltpu.make_async_copy(w_hbm.at[:, my_cols], w_mine.at[my_rows], w_load)
    w_copy.start()
    for n, src in enumerate((gate_hbm, gate_tan_hbm)):
        copy = pltpu.make_async_copy(src, gates.at[pl.ds(n, 1)], g_load.at[n])
        copy.start()
        loads.append(copy)
    s_copy = pltpu.make_async_copy(scale_hbm, scale_ref, s_load)
    s_copy.start()

    @pl.when(c == 0)
    def _():
        pl.semaphore_wait(barrier, 9)
        pl.semaphore_signal(go_clip, inc=1, device_id=c_peer, device_id_type=MESH)

    @pl.when(c == 1)
    def _():
        pl.semaphore_wait(go_clip, 1)


    sent = []

    def remote(src, dst, send_sem, recv_sem, peer):
        copy = pltpu.make_async_remote_copy(
            src_ref=src, dst_ref=dst, send_sem=send_sem, recv_sem=recv_sem,
            device_id=peer, device_id_type=MESH,
        )
        copy.start()
        sent.append(copy)
        return copy

    x_in, q_in, y_in, c_in, d_in, r_in = {}, {}, {}, {}, {}, {}

    last = (PER - 1, ORDER[-1])
    tails = []

    def keys_from(i, j, place, start=0, size=ROWS):
        return kv.at[i, j, pl.ds(place * ROWS + start, size)]

    def forward(i, j):
        own = keys_from(i, j, OWN)
        size = ROWS if (i, j) != last else SPLIT
        y_in[i, j] = remote(
            keys_from(i, j, OWN, 0, size), keys_from(i, j, ACROSS, 0, size),
            ys.at[i, j], yr.at[i, j], y_peer,
        )
        if (i, j) == last:
            for n, (place, peer) in enumerate(((ACROSS, y_peer), (DIAGONAL, diagonal))):
                tails.append(
                    remote(
                        keys_from(i, j, OWN, SPLIT, ROWS - SPLIT),
                        keys_from(i, j, place, SPLIT, ROWS - SPLIT), fs.at[n], fr.at[n], peer,
                    )
                )
        c_in[i, j] = remote(own, keys_from(i, j, MATE), cs.at[i, j], cr.at[i, j], c_peer)

    def relay(i, j):
        size = ROWS if (i, j) != last else SPLIT
        y_in[i, j].wait_recv()
        d_in[i, j] = remote(
            keys_from(i, j, ACROSS, 0, size), keys_from(i, j, DIAGONAL, 0, size),
            ds.at[i, j], dr.at[i, j], c_peer,
        )

    def columns(i, j):
        head = PER * ((x + j) % NX) + i
        return pl.ds(pl.multiple_of(head * HEAD, HEAD), HEAD)

    def send_keys(i, j):
        cols = columns(i, j)
        normed, moved = unit_rows(
            raw[0, :, cols].astype(jnp.float32), raw[1, :, cols].astype(jnp.float32)
        )
        dst = kv.at[i, 0, pl.ds(0, ROWS)] if j == 0 else kv_send.at[i, j - 1]
        dst[:, 0:128] = normed
        dst[:, 128:256] = moved
        dst[:, 256:384] = raw[2, :, cols]
        dst[:, 384:512] = raw[3, :, cols]
        if j == 0:
            forward(i, 0)
        else:
            x_in[i, j] = remote(
                dst, kv.at[i, j, pl.ds(0, ROWS)], xs.at[i, j], xr.at[i, j], at_x(j)
            )

    def send_queries(i, j):
        cols = columns(i, j)
        normed, moved = unit_rows(
            raw[4, :, cols].astype(jnp.float32), raw[5, :, cols].astype(jnp.float32)
        )
        dst = qb.at[i, pl.ds(0, ROWS)] if j == 0 else q_send.at[i, j - 1]
        dst[:, 0:128] = moved
        dst[:, 128:256] = normed
        if j != 0:
            q_in[i, j] = remote(
                dst, qb.at[i, pl.ds(j * ROWS, ROWS)], qs.at[i, j], qr.at[i, j], at_x(j)
            )

    def piece(distance, other):
        row = (((z + distance + 8) % 8) * 2 + (1 - yh if other else yh)) * DP_ROWS
        return w_mine.at[pl.ds(pl.multiple_of(row, DP_ROWS), DP_ROWS)], w_other.at[
            pl.ds(pl.multiple_of(row, DP_ROWS), DP_ROWS)
        ]

    up_in, down_in, w_in = {}, {}, []

    def w_send(distance, other, going):
        if going > 0:
            n = 2 * distance + other
            here = piece(-distance, other)[0]
            up_in[n] = remote(here, here, ps.at[n], pr.at[n], z_up)
        else:
            n = 2 * distance + other if distance < 3 else 6
            here = piece(distance, other)[0]
            down_in[n] = remote(here, here, ms.at[n], mr.at[n], z_down)

    def w_share(distance, other, n):
        here, there = piece(distance, other)
        w_in.append(remote(here, there, ws.at[n], wr.at[n], c_peer))

    def w_pass(n):
        up_in[n].wait_recv()
        down_in[n].wait_recv()
        distance, other = n // 2 + 1, n % 2
        if n < 5:
            w_send(distance, other, 1)
        if n < 4:
            w_send(distance, other, -1)
        if n == 5:
            w_send(3, 1, -1)
        w_share(-distance, other, 2 + n)
        w_share(distance, other if n < 6 else 1, 9 + n)

    for n in range(4):
        loads[n].wait()
    for j in ORDER:
        send_keys(0, j)
    loads[4].wait()
    loads[5].wait()
    for j in ORDER:
        send_queries(0, j)

    for i in range(1, PER):
        send_keys(i, 0)

    @pl.when(c == 1)
    def _():
        pl.semaphore_wait(barrier, 6)
        pl.semaphore_signal(go_w, inc=1, device_id=c_peer, device_id_type=MESH)

    @pl.when(c == 0)
    def _():
        pl.semaphore_wait(go_w, 1)

    w_copy.wait()
    outer_in = remote(w_mine.at[my_rows], w_mine.at[my_rows], os, orr, outer)
    w_send(0, 0, 1)
    w_send(0, 0, -1)
    w_share(0, 0, 0)
    for i in range(1, PER):
        for j in ORDER[1:]:
            send_keys(i, j)
        for j in ORDER:
            send_queries(i, j)

    steps = [(i, j) for i in range(PER) for j in ORDER]
    passed = 0

    def pass_up_to(n):
        nonlocal passed
        while passed < min(n, len(steps)):
            i, j = steps[passed]
            if j != 0:
                x_in[i, j].wait_recv()
                forward(i, j)
            passed += 1

    def attend(i, j, first, count, start=0, size=KEYS):
        keys, rows = pl.ds(first, count), pl.ds(start, size)
        scale = scale_ref[PER * x + i] * (1.0 / math.sqrt(HEAD))
        rate = scale * math.log2(math.e)

        scores = lax.dot_general(
            qb[i, rows, 128:256], kv[i, j, keys, 0:128], NT, preferred_element_type=jnp.float32
        )
        slopes = lax.dot_general(
            qb[i, rows, :], kv[i, j, keys, 0:256], NT, preferred_element_type=jnp.float32
        )
        probs = jnp.exp2(scores * rate)
        weighted = probs * (slopes * scale)
        p_sum = probs[:, 0:128]
        w_sum = weighted[:, 0:128]
        for part in range(1, count // 128):
            p_sum = p_sum + probs[:, part * 128 : (part + 1) * 128]
            w_sum = w_sum + weighted[:, part * 128 : (part + 1) * 128]
        p_mix = jnp.dot(
            probs.astype(jnp.bfloat16), kv[i, j, keys, 256:512], preferred_element_type=jnp.float32
        )
        w_mix = jnp.dot(
            weighted.astype(jnp.bfloat16), kv[i, j, keys, 256:384], preferred_element_type=jnp.float32
        )
        if j == 0:
            tot[rows, :] = p_sum
            mom[rows, :] = w_sum
            pv[rows, :] = p_mix
            uv[rows, :] = w_mix
        else:
            tot[rows, :] += p_sum
            mom[rows, :] += w_sum
            pv[rows, :] += p_mix
            uv[rows, :] += w_mix

    def finish(i, parts=(2, 1, 3, 0)):
        for j in parts:
            rows = pl.ds(j * ROWS, ROWS)
            inv = 1.0 / jnp.sum(tot[rows, :], -1, keepdims=True)
            moment = jnp.sum(mom[rows, :], -1, keepdims=True) * inv
            mixed = pv[rows, 0:128]
            main = (mixed * inv).astype(jnp.bfloat16)
            tangent = ((uv[rows, :] + pv[rows, 128:256] - mixed * moment) * inv).astype(jnp.bfloat16)
            if j == 0:
                att[i, x, 0:ROWS, :] = main
                att[i, x, ROWS : 2 * ROWS, :] = tangent
            else:
                ret[i, j - 1, 0:ROWS, :] = main
                ret[i, j - 1, ROWS : 2 * ROWS, :] = tangent
                r_in[i, j] = remote(
                    ret.at[i, j - 1], att.at[i, x], rs.at[i, j], rr.at[i, j], at_x(NX - j)
                )

    s_copy.wait()
    outer_in.wait_recv()
    w_send(0, 1, 1)
    w_send(0, 1, -1)
    w_share(0, 1, 1)
    pass_up_to(AHEAD)
    relay(*steps[0])
    for n, (i, j) in enumerate(steps):
        pass_up_to(n + 1 + AHEAD)
        for arrival in W_PLAN.get(n, ()):
            w_pass(arrival)
        if n + 1 < len(steps):
            relay(*steps[n + 1])
        if j == 0:
            for other in ORDER[1:]:
                q_in[i, other].wait_recv()
        c_in[i, j].wait_recv()
        if (i, j) == last:
            attend(i, j, 0, KEYS // 2)
            d_in[i, j].wait_recv()
            for copy in tails:
                copy.wait_recv()
            for parts in ((2, 3), (1, 0)):
                attend(i, j, KEYS // 2, KEYS // 2, min(parts) * ROWS, KEYS // 2)
                finish(i, parts)
        else:
            d_in[i, j].wait_recv()
            attend(i, j, 0, KEYS)
        if j == ORDER[-1] and i < PER - 1:
            finish(i)

    w_pass(6)
    loads[6].wait()
    loads[7].wait()

    def product(half, col, heads):
        pairs = [(i, k) for k in range(NX) for i in heads]
        rows = [half[pl.ds((PER * k + i) * HEAD, HEAD), pl.ds(col, 256)] for i, k in pairs]
        return jnp.dot(
            jnp.concatenate([att[i, k] for i, k in pairs], 1), jnp.concatenate(rows, 0),
            preferred_element_type=jnp.float32,
        )

    for copy in w_in:
        copy.wait_recv()
    for i in range(PER - 1):
        for j in ORDER[1:]:
            r_in[i, j].wait_recv()
    for n, half in enumerate((w_mine, w_other)):
        for col in range(0, HALF, 256):
            part[n, :, col : col + 256] = product(half, col, (0, 1))
    for j in ORDER[1:]:
        r_in[PER - 1, j].wait_recv()
    for n, (half, offset) in enumerate(((w_mine, c), (w_other, 1 - c))):
        for col in range(0, HALF, 256):
            projected = part[n, :, col : col + 256] + product(half, col, (2,))
            cols = pl.ds(pl.multiple_of(offset * HALF + col, 256), 256)
            gate, gate_tan = gates[0:1, cols], gates[1:2, cols]
            out_ref[:, cols] = gate * projected[0:ROWS]
            tan_ref[:, cols] = gate_tan * projected[0:ROWS] + gate * projected[ROWS:]
    for copy in sent:
        copy.wait_send()


def attention(q_raw, q_tan, k_raw, k_tan, values, values_tan, w_out, gate, gate_tan, head_scale):
    bf16, f32 = jnp.bfloat16, jnp.float32
    dma = pltpu.SemaphoreType.DMA
    any_spec = pl.BlockSpec(memory_space=pl.ANY)
    return pl.pallas_call(
        body,
        out_shape=[jax.ShapeDtypeStruct((ROWS, HD), f32)] * 2,
        in_specs=[any_spec] * 10,
        out_specs=[pl.BlockSpec(memory_space=pltpu.VMEM)] * 2,
        scratch_shapes=[
            pltpu.VMEM((6, ROWS, HD), bf16),
            pltpu.VMEM((2, HD), f32),
            pltpu.SMEM((HEADS,), f32),
            pltpu.VMEM((PER, NX, KEYS, 512), bf16),
            pltpu.VMEM((PER, NX - 1, ROWS, 512), bf16),
            pltpu.VMEM((PER, KEYS, 256), bf16),
            pltpu.VMEM((PER, NX - 1, ROWS, 256), bf16),
            pltpu.VMEM((KEYS, 256), f32),
            pltpu.VMEM((KEYS, 128), f32),
            pltpu.VMEM((KEYS, 128), f32),
            pltpu.VMEM((KEYS, 128), f32),
            pltpu.VMEM((PER, NX - 1, 2 * ROWS, HEAD), bf16),
            pltpu.VMEM((PER, NX, 2 * ROWS, HEAD), bf16),
            pltpu.VMEM((2, 2 * ROWS, HALF), f32),
            pltpu.VMEM((HD, HALF), bf16),
            pltpu.VMEM((HD, HALF), bf16),
            dma((6,)),
        ]
        + [dma((PER, NX))] * 12
        + [dma((2,)), dma((2,))]
        + [pltpu.SemaphoreType.REGULAR] * 2
        + [dma((2,)), dma, dma, dma, dma]
        + [dma((7,)), dma((7,)), dma((7,)), dma((7,)), dma((16,)), dma((16,))],
        compiler_params=pltpu.CompilerParams(
            collective_id=0, has_side_effects=True, vmem_limit_bytes=48 * 1024 * 1024
        ),
        cost_estimate=pl.CostEstimate(
            flops=7_000_000_000, bytes_accessed=10_000_000, transcendentals=3_200_000
        ),
        name="attention",
    )(q_raw, q_tan, k_raw, k_tan, values, values_tan, w_out, gate, gate_tan, head_scale)


def shards(q_raw, q_tan, k_raw, k_tan, values, values_tan, head_scale, w_out, gate, gate_tan):
    arrays = (q_raw, q_tan, k_raw, k_tan, values, values_tan, w_out, gate, gate_tan, head_scale)
    main, tangent = attention(
        *(pltpu.with_memory_space_constraint(array, pltpu.HBM) for array in arrays)
    )
    return (main.astype(jnp.bfloat16)[None], tangent.astype(jnp.bfloat16)[None])


def solution(mesh):
    rows = P("dp", "blk", None)
    return jax.shard_map(
        shards,
        mesh=mesh,
        in_specs=(rows,) * 6 + (P(), P("dp", None), P("dp", None), P("dp", None)),
        out_specs=(rows, rows),
        check_vma=False,
    )
```
